128 devices in a mesh: gy: 16 (over z, y_lo, core), gx: 8 (over x, y_hi).
Axes of the slice: x: 4, y: 4 (y_hi: 2, y_lo: 2; y = y_hi * 2 + y_lo), z: 4, core: 2. Of those that a mesh axis runs over, the one named last changes fastest.
Arguments:
- mean_util: float32 [32, 128, 256], P(None, 'gy', 'gx'), may hold values from -4 to 4
- observed_shares: float32 [32, 128, 256], P(None, 'gy', 'gx'), may hold values from 0.002 to 0.02
- characteristics: float32 [4, 32, 128, 256], P(None, None, 'gy', 'gx'), may hold values from -2 to 2
- taste_draws: float32 [4, 512], replicated, may hold values from -4 to 4
- taste_scale: float32 [4], replicated, may hold values from 0.3 to 1
- prior_probs: bfloat16 [32, 128, 256, 512], P(None, 'gy', 'gx'), may hold values from 0 to 0.099609375
- spill_rate: float32 [32], replicated, may hold values from 1 to 8
- utility_rate: float32 [32], replicated, may hold values from 0.1 to 0.6
- adjacency: int32 [4, 128, 256], P(None, 'gy', 'gx'), may hold values from 0 to 3
Outputs:
- final_util: float32 [32, 128, 256], P(None, 'gy', 'gx')
- log_shares: float32 [32, 128, 256], P(None, 'gy', 'gx')
- residual_max: float32 [3], replicated
The draws below stay inside these ranges and needn't reach their ends.
All inputs are finite; a program needn't handle non-finite values. Where the reference program divides by a largest or mean magnitude, that divisor is 1e-20 or more.
Results may differ from the reference program's by a relative error of at most 0.0008.
Values may be sent and summed in bfloat16 or wider, within the bound.
A program may use at most 192 MiB of HBM per device.

```python
import math
import jax
import jax.numpy as jnp
from jax import lax

J = 32
K = 4
R = 512
ITERS = 3
NROWS = 128
NCOLS = 256


def place_ends(values, key, low, top_value):
    index_at = [jax.random.randint(jax.random.fold_in(key, axis), (), 0, length) for axis, length in enumerate(values.shape)]
    longest = values.shape.index(max(values.shape))
    neighbour = index_at[:longest] + [(index_at[longest] + 1) % values.shape[longest]] + index_at[longest + 1:]
    return values.at[tuple(index_at)].set(low).at[tuple(neighbour)].set(top_value)


def block_scale(stream_key, extent, cuts, smallest, largest):
    def one(dim, blocks):
        heights = jax.random.uniform(jax.random.fold_in(jax.random.fold_in(stream_key, 6), dim), (blocks,), jnp.float32, smallest / len(cuts), largest / len(cuts))
        return jnp.repeat(jnp.exp(heights), extent[dim] // blocks).reshape((-1,) + (1,) * (len(extent) - dim - 1))

    gain = one(*cuts[0])
    for cut in cuts[1:]:
        gain = gain * one(*cut)
    return gain


def normal_values(own_key, shape, width, most, pieces=(), held_as=jnp.bfloat16):
    values = width * jax.random.normal(own_key, shape, jnp.float32)
    if pieces:
        values = values * block_scale(own_key, shape, pieces, -0.22, 0.18)
    return jnp.clip(values, -most, most).astype(held_as)


def setup_inputs(seed: int = 0) -> dict:
    splits = jax.random.split(jax.random.key(seed), 10)
    return {
        "mean_util": normal_values(splits[0], (J, NROWS, NCOLS), 1.0, 4.0, ((1, 16), (2, 8)), jnp.float32),
        "observed_shares": jnp.clip(jnp.exp(math.log(0.02) - 2.30258502 * jax.random.uniform(splits[1], (J, NROWS, NCOLS), jnp.float32) ** block_scale(splits[1], (J, NROWS, NCOLS), ((1, 16), (2, 8)), -0.2, 0.2)), 0.002, 0.02),
        "characteristics": normal_values(splits[2], (K, J, NROWS, NCOLS), 0.7, 2.0, ((2, 16), (3, 8)), jnp.float32),
        "taste_draws": normal_values(splits[3], (K, R), 1.0, 4.0, (), jnp.float32),
        "taste_scale": jnp.clip(jnp.exp(jax.random.uniform(splits[4], (K,), jnp.float32, math.log(0.3), math.log(1.0))), 0.3, 1.0),
        "prior_probs": jnp.clip(0.099609375 * jax.random.uniform(splits[5], (J, NROWS, NCOLS, R), jnp.float32) ** block_scale(splits[5], (J, NROWS, NCOLS, R), ((1, 16), (2, 8)), -0.2, 0.2), 0.0, 0.099609375).astype(jnp.bfloat16),
        "spill_rate": jnp.clip(jnp.exp(jax.random.uniform(splits[6], (J,), jnp.float32, math.log(1.0), math.log(8.0))), 1.0, 8.0),
        "utility_rate": jnp.clip(jax.random.uniform(splits[7], (J,), jnp.float32, 0.1, 0.6), 0.1, 0.6),
        "adjacency": place_ends(jax.random.randint(splits[8], (4, NROWS, NCOLS), 0, 4), jax.random.fold_in(splits[8], 1), 0, 3).astype(jnp.int32),
    }


step_level = 0.2
gap_eps = 1e-6


def neighbour_avg(padded, link_weights, inverse):
    north_side = padded[:, :-2, 1:-1]
    south_side = padded[:, 2:, 1:-1]
    west_side = padded[:, 1:-1, :-2]
    east_side = padded[:, 1:-1, 2:]
    summed = link_weights[0] * north_side + link_weights[1] * south_side
    summed = summed + link_weights[2] * west_side + link_weights[3] * east_side
    return summed * inverse


def reference(mean_util, observed_shares, characteristics, taste_draws, taste_scale, prior_probs, spill_rate, utility_rate, adjacency):
    link_weights = adjacency.astype(jnp.float32)
    inverse = 1.0 / jnp.maximum(jnp.sum(link_weights, axis=0), 1.0)
    log_observed = jnp.log(observed_shares)
    scaled_chars = characteristics * taste_scale[:, None, None, None]
    draws_state = (spill_rate[:, None, None, None] * prior_probs).astype(jnp.bfloat16)
    draws_state = jnp.transpose(draws_state, (1, 0, 2, 3))
    worst_list = []
    log_pred = mean_util
    for iteration in range(ITERS):
        util_padded = jnp.pad(mean_util, ((0, 0), (1, 1), (1, 1)))
        base_util = mean_util + utility_rate[:, None, None] * neighbour_avg(util_padded, link_weights, inverse)
        draws_padded = jnp.pad(draws_state, ((1, 1), (0, 0), (1, 1), (0, 0)))

        def one_row(row_index):
            rows_three = lax.dynamic_slice_in_dim(draws_padded, row_index, 3, 0)
            row_weights = lax.dynamic_slice_in_dim(link_weights, row_index, 1, 1)[:, 0][:, :, None]
            row_inverse = lax.dynamic_slice_in_dim(inverse, row_index, 1, 0)[0][:, None]
            north_side = rows_three[0][:, 1:-1]
            south_side = rows_three[2][:, 1:-1]
            west_side = rows_three[1][:, :-2]
            east_side = rows_three[1][:, 2:]
            spill = row_weights[0] * north_side + row_weights[1] * south_side
            spill = (spill + row_weights[2] * west_side + row_weights[3] * east_side) * row_inverse
            row_chars = lax.dynamic_slice_in_dim(scaled_chars, row_index, 1, 2)[:, :, 0]
            taste_part = jnp.einsum('kjc,kr->jcr', row_chars, taste_draws, precision=lax.Precision.HIGHEST)
            row_base = lax.dynamic_slice_in_dim(base_util, row_index, 1, 1)[:, 0]
            utility = row_base[:, :, None] + taste_part + spill
            exponent = jnp.exp(utility)
            denominator = 1.0 + jnp.sum(exponent, axis=0)
            choice_prob = exponent / denominator
            new_state = (spill_rate[:, None, None] * choice_prob).astype(jnp.bfloat16)
            return jnp.mean(choice_prob, axis=-1), new_state

        row_shares, draws_state = lax.map(one_row, jnp.arange(NROWS, dtype=jnp.int32))
        log_pred = jnp.log(jnp.transpose(row_shares, (1, 0, 2)))
        residual = log_observed - log_pred
        worst_gap = jnp.max(jnp.abs(residual))
        step_size = step_level / (worst_gap + gap_eps)
        mean_util = mean_util + step_size * residual
        worst_list.append(worst_gap)
    return mean_util, log_pred, jnp.stack(worst_list)
```

```python
import functools
import math

import jax
import jax.numpy as jnp
from jax import lax
from jax.experimental import pallas as pl
from jax.experimental.pallas import tpu as pltpu
from jax.sharding import PartitionSpec as P

ITERS = 3
J = 32
K = 4
TR = 8
TC = 32
M = TR * TC
HM = M // 2
R = 512
RC = 128
NC = R // RC
NY = 16
NX = 8
LOG2E = math.log2(math.e)
step_level = 0.2
gap_eps = 1e-06
MESH = pl.DeviceIdType.MESH
F32 = jnp.float32
BF16 = jnp.bfloat16


def lane_iota(shape):
    return lax.broadcasted_iota(jnp.int32, shape, len(shape) - 1)


def row_iota(shape):
    return lax.broadcasted_iota(jnp.int32, shape, len(shape) - 2)


def exact_dot(a, b, dims):
    return lax.dot_general(
        a, b, (dims, ((), ())), precision=lax.Precision.HIGHEST, preferred_element_type=F32
    )


def kernel(
    mean_in, obs_in, chars_in, draws_ref, scale_ref, prior_in, spill_ref, rate_ref, adj_ref,
    mean_out, log_out, gap_out,
    st, hr, hc, cs, taste, ex, bx, den, rden, amat, aw, inv, gain, cz, char_buf,
    zmean, zobs, zlog, zsend, zc_send, hz_r, hz_c, mh_r, mh_c, share, mxs, mxg, mxy,
    prior_sem, char_sem, s_sem, r_sem, sz_sem, rz_sem, sg_sem, rg_sem, sy_sem, ry_sem,
):
    gy = lax.axis_index("gy")
    gx = lax.axis_index("gx")

    def prior_copy(c):
        return pltpu.make_async_copy(
            prior_in.at[:, :, :, pl.ds(pl.multiple_of(c * RC, RC), RC)], st.at[0, c], prior_sem.at[c]
        )

    for c in range(NC):
        prior_copy(c).start()
    char_copy = pltpu.make_async_copy(chars_in, char_buf, char_sem)
    char_copy.start()

    barrier = pltpu.get_barrier_semaphore()
    for d in range(1, NX):
        pl.semaphore_signal(
            barrier, inc=1, device_id={"gx": lax.rem(gx + d, NX)}, device_id_type=MESH
        )
    for d in range(1, NY):
        pl.semaphore_signal(
            barrier, inc=1, device_id={"gy": lax.rem(gy + d, NY)}, device_id_type=MESH
        )
    pl.semaphore_wait(barrier, NX - 1 + NY - 1)

    north = {"gy": lax.rem(gy + NY - 1, NY)}
    south = {"gy": lax.rem(gy + 1, NY)}
    west = {"gx": lax.rem(gx + NX - 1, NX)}
    east = {"gx": lax.rem(gx + 1, NX)}

    def edge_copies(e, c):
        b = e % 2
        plan = (
            (st.at[b, c, :, TR - 1], hr.at[e, c, 0], south),
            (st.at[b, c, :, 0], hr.at[e, c, 1], north),
            (cs.at[e, c, 1], hc.at[e, c, 0], east),
            (cs.at[e, c, 0], hc.at[e, c, 1], west),
        )
        return [
            pltpu.make_async_remote_copy(
                src_ref=src, dst_ref=dst, send_sem=s_sem.at[e, c, k], recv_sem=r_sem.at[e, c, k],
                device_id=to, device_id_type=MESH,
            )
            for k, (src, dst, to) in enumerate(plan)
        ]

    def small_copies(x):
        plan = (
            (zsend.at[x, pl.ds(M - TC, TC)], hz_r.at[x, 0], south),
            (zsend.at[x, pl.ds(0, TC)], hz_r.at[x, 1], north),
            (zc_send.at[x, 1], hz_c.at[x, 0], east),
            (zc_send.at[x, 0], hz_c.at[x, 1], west),
        )
        return [
            pltpu.make_async_remote_copy(
                src_ref=src, dst_ref=dst, send_sem=sz_sem.at[x, k], recv_sem=rz_sem.at[x, k],
                device_id=to, device_id_type=MESH,
            )
            for k, (src, dst, to) in enumerate(plan)
        ]

    def send_small(x, value):
        zsend[x] = value
        zc_send[x, 0] = zsend[x, pl.ds(0, TR, stride=TC), :]
        zc_send[x, 1] = zsend[x, pl.ds(TC - 1, TR, stride=TC), :]
        for copy in small_copies(x):
            copy.start()

    @pl.loop(0, NC)
    def _(c):
        prior_copy(c).wait()

        @pl.loop(0, J // 2)
        def _(q):
            west_cols = []
            east_cols = []
            for jj in range(2):
                j = 2 * q + jj
                value = st[0, c, j].reshape(M, RC).astype(F32) * spill_ref[j]
                st[0, c, j] = value.astype(BF16).reshape(TR, TC, RC)
                ex[j] = value
                west_cols.append(ex[j, pl.ds(0, TR, stride=TC), :])
                east_cols.append(ex[j, pl.ds(TC - 1, TR, stride=TC), :])
            cs[0, c, 0, q] = jnp.concatenate(west_cols, axis=0).astype(BF16)
            cs[0, c, 1, q] = jnp.concatenate(east_cols, axis=0).astype(BF16)

        for copy in edge_copies(0, c):
            copy.start()

    eye = (row_iota((TC, TC)) == lane_iota((TC, TC))).astype(F32)
    eye_wide = (row_iota((J, 128)) == lane_iota((J, 128))).astype(F32)
    pad = jnp.zeros((128 - J, TC), F32)

    def to_markets(block):
        return exact_dot(eye, jnp.concatenate([block, pad], axis=0), ((1,), (1,)))

    for row in range(TR):
        rows = pl.ds(row * TC, TC)
        zmean[rows, :] = to_markets(mean_in[:, row, :])
        zobs[rows, :] = to_markets(jnp.log(obs_in[:, row, :]))
    send_small(0, zmean[...])

    for k in range(4):
        for row in range(TR):
            line = adj_ref[k, pl.ds(row, 1), :].astype(F32)
            column = jnp.sum(jnp.where(eye > 0, line, 0.0), axis=1, keepdims=True)
            aw[k, pl.ds(row * TC, TC), :] = jnp.broadcast_to(column, (TC, 128))
    links = jnp.maximum(aw[0] + aw[1] + aw[2] + aw[3], 1.0)
    inverse = 1.0 / links
    inv[...] = inverse
    gain[...] = inverse * LOG2E

    @pl.loop(0, 4)
    def _(i):
        par = i // 2
        h = i % 2
        shape = (HM, 128)
        at = row_iota(shape)
        col = at & (TC - 1)
        row = (at >> 5) + h * (TR // 2)
        mrows = pl.ds(pl.multiple_of(h * HM, HM), HM)
        w0 = jnp.where((row == 0) & (gy == 0), 0.0, aw[0, mrows, :])
        w1 = jnp.where((row == TR - 1) & (gy == NY - 1), 0.0, aw[1, mrows, :])
        w2 = jnp.where((col == 0) & (gx == 0), 0.0, aw[2, mrows, :])
        w3 = jnp.where((col == TC - 1) & (gx == NX - 1), 0.0, aw[3, mrows, :])
        west_slot = jnp.where(col == 0, 192 + par * TR + row, at + TC - 1)
        east_slot = jnp.where(col == TC - 1, 208 + par * TR + row, at + TC + 1)
        for part in range(2):
            slot = lane_iota(shape) + part * 128
            entry = jnp.where(slot == at, w0, 0.0)
            entry = entry + jnp.where(slot == at + 2 * TC, w1, 0.0)
            entry = entry + jnp.where(slot == west_slot, w2, 0.0)
            entry = entry + jnp.where(slot == east_slot, w3, 0.0)
            amat[par, h, :, pl.ds(part * 128, 128)] = entry.astype(BF16)

    char_copy.wait()

    @pl.loop(0, K)
    def _(k):
        for row in range(TR):
            cz[k, pl.ds(row * TC, TC), :] = to_markets(char_buf[k, :, row, :])

    draw_rows = [
        [draws_ref[pl.ds(k, 1), pl.ds(c * RC, RC)] * (scale_ref[k] * LOG2E) for c in range(NC)]
        for k in range(K)
    ]

    @pl.loop(0, J)
    def _(j):
        @pl.loop(0, TR)
        def _(row):
            rows = pl.ds(pl.multiple_of(row * TC, TC), TC)
            here = lane_iota((TC, 128)) == j
            columns = [
                jnp.sum(jnp.where(here, cz[k, rows, :], 0.0), axis=1, keepdims=True) for k in range(K)
            ]
            for c in range(NC):
                total = columns[0] * draw_rows[0][c]
                for k in range(1, K):
                    total = total + columns[k] * draw_rows[k][c]
                taste[c, j, rows, :] = total

    rates = jnp.zeros((1, 128), F32)
    for j in range(J):
        rates = jnp.where(lane_iota((1, 128)) == j, rate_ref[j], rates)
    real = lane_iota((M, 128)) < J
    zero_rows = jnp.zeros((TR, 128), F32)
    zero_tail = jnp.zeros((32, 128), F32)

    def largest(t, value):
        mxs[t, 0] = value
        mxg[t, gx] = value

        def along_x(d):
            return pltpu.make_async_remote_copy(
                src_ref=mxs.at[t, 0], dst_ref=mxg.at[t, gx], send_sem=sg_sem.at[t, d],
                recv_sem=rg_sem.at[t, gx], device_id={"gx": lax.rem(gx + d, NX)}, device_id_type=MESH,
            )

        def from_x(d):
            k = lax.rem(gx + d, NX)
            return pltpu.make_async_remote_copy(
                src_ref=mxs.at[t, 0], dst_ref=mxg.at[t, k], send_sem=sg_sem.at[t, d],
                recv_sem=rg_sem.at[t, k], device_id={"gx": k}, device_id_type=MESH,
            )

        def along_y(d):
            return pltpu.make_async_remote_copy(
                src_ref=mxs.at[t, 1], dst_ref=mxy.at[t, gy], send_sem=sy_sem.at[t, d],
                recv_sem=ry_sem.at[t, gy], device_id={"gy": lax.rem(gy + d, NY)}, device_id_type=MESH,
            )

        def from_y(d):
            k = lax.rem(gy + d, NY)
            return pltpu.make_async_remote_copy(
                src_ref=mxs.at[t, 1], dst_ref=mxy.at[t, k], send_sem=sy_sem.at[t, d],
                recv_sem=ry_sem.at[t, k], device_id={"gy": k}, device_id_type=MESH,
            )

        for d in range(1, NX):
            along_x(d).start()
        for d in range(1, NX):
            from_x(d).wait_recv()
        best = mxg[t, 0]
        for k in range(1, NX):
            best = jnp.maximum(best, mxg[t, k])
        mxs[t, 1] = best
        mxy[t, gy] = best
        for d in range(1, NY):
            along_y(d).start()
        for d in range(1, NY):
            from_y(d).wait_recv()
        best = mxy[t, 0]
        for k in range(1, NY):
            best = jnp.maximum(best, mxy[t, k])
        for d in range(1, NX):
            along_x(d).wait_send()
        for d in range(1, NY):
            along_y(d).wait_send()
        return best

    for copy in small_copies(0):
        copy.wait()
    mh_r[...] = hz_r[0]
    mh_c[...] = hz_c[0]

    for t in range(ITERS):
        b = t % 2
        last = t == ITERS - 1

        mean_now = zmean[...]
        west_halo = [mh_c[0], zero_rows]
        east_halo = [mh_c[1], zero_rows]
        for h in range(2):
            if h == 0:
                pieces = [mh_r[0], mean_now[: 5 * TC]]
            else:
                pieces = [mean_now[3 * TC :], mh_r[1]]
            around = jnp.concatenate(pieces + west_halo + east_halo + [zero_tail], axis=0)
            part = exact_dot(amat[0, h].astype(F32), around, ((1,), (0,)))
            rows = pl.ds(h * HM, HM)
            zlog[rows, :] = (zmean[rows, :] + rates * (part * inv[rows, :])) * LOG2E

        @pl.loop(0, J)
        def _(j):
            picked = jnp.where(lane_iota((M, 128)) == j, zlog[...], 0.0)
            bx[j] = jnp.broadcast_to(jnp.sum(picked, axis=1, keepdims=True), (M, 128))

        share[...] = jnp.zeros((M, 128), F32)

        @pl.loop(0, NC)
        def _(c):
            for copy in edge_copies(t, c):
                copy.wait_recv()
            den[...] = jnp.ones((M, RC), F32)

            @pl.loop(0, J // 2)
            def _(q):
                halo_cols = [hc[t, c, 0, q], hc[t, c, 1, q], jnp.zeros((32, RC), BF16)]
                for h in range(2):
                    rows = pl.ds(h * HM, HM)
                    total = den[rows, :]
                    for jj in range(2):
                        j = 2 * q + jj
                        if h == 0:
                            pieces = [hr[t, c, 0, j], st[b, c, j, pl.ds(0, 5)].reshape(5 * TC, RC)]
                        else:
                            pieces = [st[b, c, j, pl.ds(3, 5)].reshape(5 * TC, RC), hr[t, c, 1, j]]
                        around = jnp.concatenate(pieces + halo_cols, axis=0)
                        spill = lax.dot_general(
                            amat[jj, h], around, (((1,), (0,)), ((), ())), preferred_element_type=F32
                        )
                        power = spill * gain[rows, :] + (taste[c, j, rows, :] + bx[j, rows, :])
                        value = jnp.exp2(power)
                        ex[j, rows, :] = value
                        total = total + value
                    den[rows, :] = total

            rden[...] = 1.0 / den[...]
            if t == 1:
                for copy in edge_copies(0, c):
                    copy.wait_send()

            @pl.loop(0, J // 2)
            def _(q):
                west_cols = []
                east_cols = []
                for jj in range(2):
                    j = 2 * q + jj
                    for h in range(2):
                        rows = pl.ds(h * HM, HM)
                        prob = ex[j, rows, :] * rden[rows, :]
                        here = lane_iota((HM, 128)) == j
                        share[rows, :] += jnp.where(here, jnp.sum(prob, axis=1, keepdims=True), 0.0)
                        if not last:
                            st[1 - b, c, j, pl.ds(h * (TR // 2), TR // 2)] = (
                                (prob * spill_ref[j]).astype(BF16).reshape(TR // 2, TC, RC)
                            )
                    if not last:
                        for cols, first in ((west_cols, 0), (east_cols, TC - 1)):
                            at = pl.ds(first, TR, stride=TC)
                            cols.append(ex[j, at, :] * rden[at, :] * spill_ref[j])
                if not last:
                    cs[t + 1, c, 0, q] = jnp.concatenate(west_cols, axis=0).astype(BF16)
                    cs[t + 1, c, 1, q] = jnp.concatenate(east_cols, axis=0).astype(BF16)

            if not last:
                for copy in edge_copies(t + 1, c):
                    copy.start()

        log_share = jnp.log(jnp.where(real, share[...] * (1.0 / R), 1.0))
        residual = jnp.where(real, zobs[...] - log_share, 0.0)
        if not last:
            send_small(t + 1, residual)
        gap = jnp.max(jnp.max(jnp.abs(residual), axis=0, keepdims=True), axis=1, keepdims=True)
        if last:
            for row in range(TR):
                log_out[:, row, :] = exact_dot(
                    eye_wide, log_share[row * TC : (row + 1) * TC], ((1,), (1,))
                )
        best = largest(t, jnp.broadcast_to(gap, (1, 128)))
        gap_out[t] = jnp.max(best)
        step = step_level / (best + gap_eps)
        mean_now = zmean[...] + step * residual
        if not last:
            zmean[...] = mean_now
            for copy in small_copies(t + 1):
                copy.wait()
            mh_r[...] = mh_r[...] + step * hz_r[t + 1]
            mh_c[...] = mh_c[...] + step * hz_c[t + 1]
        else:
            for row in range(TR):
                mean_out[:, row, :] = exact_dot(
                    eye_wide, mean_now[row * TC : (row + 1) * TC], ((1,), (1,))
                )

    for e in range(1, ITERS):
        @pl.loop(0, NC)
        def _(c):
            for copy in edge_copies(e, c):
                copy.wait_send()


def local(*args):
    vmem = pl.BlockSpec(memory_space=pltpu.VMEM)
    smem = pl.BlockSpec(memory_space=pltpu.SMEM)
    anyspace = pl.BlockSpec(memory_space=pl.ANY)
    dma = pltpu.SemaphoreType.DMA
    small = jax.ShapeDtypeStruct((J, TR, TC), F32)
    return pl.pallas_call(
        kernel,
        out_shape=(small, small, jax.ShapeDtypeStruct((ITERS,), F32)),
        in_specs=[vmem, vmem, anyspace, vmem, smem, anyspace, smem, smem, vmem],
        out_specs=(vmem, vmem, smem),
        scratch_shapes=[
            pltpu.VMEM((2, NC, J, TR, TC, RC), BF16),
            pltpu.VMEM((ITERS, NC, 2, J, TC, RC), BF16),
            pltpu.VMEM((ITERS, NC, 2, J // 2, 2 * TR, RC), BF16),
            pltpu.VMEM((ITERS, NC, 2, J // 2, 2 * TR, RC), BF16),
            pltpu.VMEM((NC, J, M, RC), F32),
            pltpu.VMEM((J, M, RC), F32),
            pltpu.VMEM((J, M, 128), F32),
            pltpu.VMEM((M, RC), F32),
            pltpu.VMEM((M, RC), F32),
            pltpu.VMEM((2, 2, HM, 256), BF16),
            pltpu.VMEM((4, M, 128), F32),
            pltpu.VMEM((M, 128), F32),
            pltpu.VMEM((M, 128), F32),
            pltpu.VMEM((K, M, 128), F32),
            pltpu.VMEM((K, J, TR, TC), F32),
            pltpu.VMEM((M, 128), F32),
            pltpu.VMEM((M, 128), F32),
            pltpu.VMEM((M, 128), F32),
            pltpu.VMEM((ITERS, M, 128), F32),
            pltpu.VMEM((ITERS, 2, TR, 128), F32),
            pltpu.VMEM((ITERS, 2, TC, 128), F32),
            pltpu.VMEM((ITERS, 2, TR, 128), F32),
            pltpu.VMEM((2, TC, 128), F32),
            pltpu.VMEM((2, TR, 128), F32),
            pltpu.VMEM((M, 128), F32),
            pltpu.VMEM((ITERS, 2, 1, 128), F32),
            pltpu.VMEM((ITERS, NX, 1, 128), F32),
            pltpu.VMEM((ITERS, NY, 1, 128), F32),
            dma((NC,)),
            dma,
            dma((ITERS, NC, 4)),
            dma((ITERS, NC, 4)),
            dma((ITERS, 4)),
            dma((ITERS, 4)),
            dma((ITERS, NX)),
            dma((ITERS, NX)),
            dma((ITERS, NY)),
            dma((ITERS, NY)),
        ],
        compiler_params=pltpu.CompilerParams(
            collective_id=0, has_side_effects=True, vmem_limit_bytes=62 * 1024 * 1024
        ),
    )(*args)


def solution(mesh):
    tile = P(None, "gy", "gx")
    placed = (
        tile, tile, P(None, None, "gy", "gx"), P(), P(), P(None, "gy", "gx", None), P(), P(), tile,
    )
    return jax.shard_map(
        local, mesh=mesh, in_specs=placed, out_specs=(tile, tile, P()), check_vma=False
    )
```

```python
import functools
import math

import jax
import jax.numpy as jnp
from jax import lax
from jax.experimental import pallas as pl
from jax.experimental.pallas import tpu as pltpu
from jax.sharding import PartitionSpec as P

ITERS = 3
J = 32
K = 4
TR = 8
TC = 32
M = TR * TC
HM = M // 2
R = 512
RC = 256
NC = R // RC
NP = RC // 128
NY = 16
NX = 8
BM = 64
CUTS = (0, 24, 32)
ALL = tuple(range(len(CUTS) - 1))
LOG2E = math.log2(math.e)
step_level = 0.2
gap_eps = 1e-06
MESH = pl.DeviceIdType.MESH
F32 = jnp.float32
BF16 = jnp.bfloat16


def lane_iota(shape):
    return lax.broadcasted_iota(jnp.int32, shape, len(shape) - 1)


def row_iota(shape):
    return lax.broadcasted_iota(jnp.int32, shape, len(shape) - 2)


def exact_dot(a, b, dims):
    return lax.dot_general(
        a, b, (dims, ((), ())), precision=lax.Precision.HIGHEST, preferred_element_type=F32
    )


def kernel(
    mean_in, obs_in, chars_in, draws_ref, scale_ref, prior_in, spill_ref, rate_ref, adj_ref,
    mean_out, log_out, gap_out,
    st, hr, hc, cs, ex, den, rden, amat, near, far, lhs, chars_wide, draw_rows, aw, links, inv, gain,
    char_buf, zmean, zobs, zsend, zc_send, hz_r, hz_c, mh_r, mh_c, share, mxs, mxg, mxy,
    prior_sem, char_sem, s_sem, r_sem, sz_sem, rz_sem, sg_sem, rg_sem, sy_sem, ry_sem,
):
    gy = lax.axis_index("gy")
    gx = lax.axis_index("gx")

    def prior_copy(c):
        return pltpu.make_async_copy(
            prior_in.at[:, :, :, pl.ds(pl.multiple_of(c * RC, RC), RC)], st.at[0, c], prior_sem.at[c]
        )

    for c in range(NC):
        prior_copy(c).start()
    char_copy = pltpu.make_async_copy(chars_in, char_buf, char_sem)
    char_copy.start()

    barrier = pltpu.get_barrier_semaphore()
    for d in range(1, NX):
        pl.semaphore_signal(
            barrier, inc=1, device_id={"gx": lax.rem(gx + d, NX)}, device_id_type=MESH
        )
    for d in range(1, NY):
        pl.semaphore_signal(
            barrier, inc=1, device_id={"gy": lax.rem(gy + d, NY)}, device_id_type=MESH
        )
    pl.semaphore_wait(barrier, NX - 1 + NY - 1)

    north = {"gy": lax.rem(gy + NY - 1, NY)}
    south = {"gy": lax.rem(gy + 1, NY)}
    west = {"gx": lax.rem(gx + NX - 1, NX)}
    east = {"gx": lax.rem(gx + 1, NX)}

    def edge_copies(e, c, pieces):
        b = e % 2
        copies = []
        for p in pieces:
            js = pl.ds(CUTS[p], CUTS[p + 1] - CUTS[p])
            qs = pl.ds(CUTS[p] // 2, (CUTS[p + 1] - CUTS[p]) // 2)
            plan = (
                (st.at[b, c, js, TR - 1], hr.at[e, c, 0, js], south),
                (st.at[b, c, js, 0], hr.at[e, c, 1, js], north),
                (cs.at[e, c, 1, qs], hc.at[e, c, 0, qs], east),
                (cs.at[e, c, 0, qs], hc.at[e, c, 1, qs], west),
            )
            for k, (src, dst, to) in enumerate(plan):
                copies.append(
                    pltpu.make_async_remote_copy(
                        src_ref=src, dst_ref=dst, send_sem=s_sem.at[e, c, p, k],
                        recv_sem=r_sem.at[e, c, p, k], device_id=to, device_id_type=MESH,
                    )
                )
        return copies

    def small_copies(x):
        plan = (
            (zsend.at[x, pl.ds(M - TC, TC)], hz_r.at[x, 0], south),
            (zsend.at[x, pl.ds(0, TC)], hz_r.at[x, 1], north),
            (zc_send.at[x, 1], hz_c.at[x, 0], east),
            (zc_send.at[x, 0], hz_c.at[x, 1], west),
        )
        return [
            pltpu.make_async_remote_copy(
                src_ref=src, dst_ref=dst, send_sem=sz_sem.at[x, k], recv_sem=rz_sem.at[x, k],
                device_id=to, device_id_type=MESH,
            )
            for k, (src, dst, to) in enumerate(plan)
        ]

    def send_small(x, value):
        zsend[x] = value
        zc_send[x, 0] = zsend[x, pl.ds(0, TR, stride=TC), :]
        zc_send[x, 1] = zsend[x, pl.ds(TC - 1, TR, stride=TC), :]
        for copy in small_copies(x):
            copy.start()

    @pl.loop(0, NC)
    def _(c):
        prior_copy(c).wait()

        @pl.loop(0, J // 2)
        def _(q):
            west_cols = []
            east_cols = []
            for jj in range(2):
                j = 2 * q + jj
                value = st[0, c, j].reshape(M, RC).astype(F32) * spill_ref[j]
                st[0, c, j] = value.astype(BF16).reshape(TR, TC, RC)
                for part in range(NP):
                    ex[j, part] = value[:, part * 128 : (part + 1) * 128]
                for cols, first in ((west_cols, 0), (east_cols, TC - 1)):
                    cols.append(
                        jnp.concatenate(
                            [
                                ex[j, part, pl.ds(first, TR, stride=TC), :]
                                for part in range(NP)
                            ],
                            axis=1,
                        )
                    )
            cs[0, c, 0, q] = jnp.concatenate(west_cols, axis=0).astype(BF16)
            cs[0, c, 1, q] = jnp.concatenate(east_cols, axis=0).astype(BF16)

        for copy in edge_copies(0, c, ALL):
            copy.start()

    eye = (row_iota((TC, TC)) == lane_iota((TC, TC))).astype(F32)
    eye_wide = (row_iota((J, 128)) == lane_iota((J, 128))).astype(F32)
    pad = jnp.zeros((128 - J, TC), F32)

    def to_markets(block):
        return exact_dot(eye, jnp.concatenate([block, pad], axis=0), ((1,), (1,)))

    for row in range(TR):
        rows = pl.ds(row * TC, TC)
        zmean[rows, :] = to_markets(mean_in[:, row, :])
        zobs[rows, :] = to_markets(jnp.log(obs_in[:, row, :]))
    send_small(0, zmean[...])

    for k in range(4):
        for row in range(TR):
            line = adj_ref[k, pl.ds(row, 1), :].astype(F32)
            column = jnp.sum(jnp.where(eye > 0, line, 0.0), axis=1, keepdims=True)
            aw[k, pl.ds(row * TC, TC), :] = jnp.broadcast_to(column, (TC, 128))
    count = jnp.maximum(aw[0] + aw[1] + aw[2] + aw[3], 1.0)
    links[...] = count
    inverse = 1.0 / count
    inv[...] = inverse
    gain[...] = jnp.concatenate([inverse * LOG2E] * (RC // 128), axis=1)

    @pl.loop(0, 2)
    def _(h):
        shape = (HM, 128)
        at = row_iota(shape)
        lane = lane_iota(shape)
        block = lane >> 5
        col = at & (TC - 1)
        row = (at >> 5) + h * (TR // 2)
        mrows = pl.ds(pl.multiple_of(h * HM, HM), HM)
        w0 = jnp.where((row == 0) & (gy == 0), 0.0, aw[0, mrows, :])
        w1 = jnp.where((row == TR - 1) & (gy == NY - 1), 0.0, aw[1, mrows, :])
        w2 = jnp.where((col == 0) & (gx == 0), 0.0, aw[2, mrows, :])
        w3 = jnp.where((col == TC - 1) & (gx == NX - 1), 0.0, aw[3, mrows, :])

        def entries(slot, par):
            west_slot = jnp.where(col == 0, 192 + par * TR + row, at + TC - 1)
            east_slot = jnp.where(col == TC - 1, 208 + par * TR + row, at + TC + 1)
            entry = jnp.where(slot == at, w0, 0.0)
            entry = entry + jnp.where(slot == at + 2 * TC, w1, 0.0)
            entry = entry + jnp.where(slot == west_slot, w2, 0.0)
            return entry + jnp.where(slot == east_slot, w3, 0.0)

        first = entries(lane, 0)
        amat[h, :, pl.ds(0, 128)] = first
        near[h] = first.astype(BF16)
        amat[h, :, pl.ds(128, 128)] = entries(lane + 128, 0)
        for i in range(4):
            slot = jnp.where(block > i, lane + 96, lane + 128)
            far[i, h] = jnp.where(block == i, 0.0, entries(slot, i % 2))

    def split(value):
        high = value.astype(BF16)
        rest = value - high.astype(F32)
        middle = rest.astype(BF16)
        return high, middle, (rest - middle.astype(F32)).astype(BF16)

    def select_sum(parts, masks):
        total = None
        for part, mask in zip(parts, masks):
            term = lax.dot_general(
                part, mask.astype(F32).astype(BF16), (((1,), (0,)), ((), ())), preferred_element_type=F32
            )
            total = term if total is None else total + term
        return total

    char_copy.wait()
    for row in range(TR):
        block = jnp.concatenate([char_buf[k, :, row, :] for k in range(K)], axis=0)
        rows = pl.ds(row * TC, TC)
        ex[0, 0, rows, :] = exact_dot(eye, block, ((1,), (1,))) * links[rows, :]
    char_parts = split(ex[0, 0])
    source = row_iota((128, 128))
    place = lane_iota((128, 128))
    within = place & 31

    @pl.loop(0, J // 4)
    def _(b):
        kept = ((source >> 5) == (within & 3)) & ((source & 31) == 4 * b + (place >> 5))
        term = within >> 2
        chars_wide[b] = select_sum(
            char_parts,
            (
                kept & ((term == 0) | (term == 1) | (term == 4)),
                kept & ((term == 2) | (term == 3)),
                kept & (term == 5),
            ),
        )

    scaled = jnp.concatenate([draws_ref[pl.ds(k, 1), :] * scale_ref[k] for k in range(K)], axis=0)
    high, middle, low = (part.astype(F32) for part in split(scaled))
    draw_rows[...] = jnp.concatenate(
        [high, middle, high, middle, low, high, jnp.ones((3, R), F32), jnp.zeros((5, R), F32)], axis=0
    ).astype(BF16)

    rates = jnp.zeros((1, 128), F32)
    for j in range(J):
        rates = jnp.where(lane_iota((1, 128)) == j, rate_ref[j], rates)
    real = lane_iota((M, 128)) < J
    zero_rows = jnp.zeros((TR, 128), F32)
    zero_tail = jnp.zeros((32, 128), F32)

    def largest(t, value, meanwhile, afterwards):
        mxs[t, 0] = value
        mxg[t, gx] = value

        def along_x(d):
            return pltpu.make_async_remote_copy(
                src_ref=mxs.at[t, 0], dst_ref=mxg.at[t, gx], send_sem=sg_sem.at[t, d],
                recv_sem=rg_sem.at[t, gx], device_id={"gx": lax.rem(gx + d, NX)}, device_id_type=MESH,
            )

        def from_x(d):
            k = lax.rem(gx + d, NX)
            return pltpu.make_async_remote_copy(
                src_ref=mxs.at[t, 0], dst_ref=mxg.at[t, k], send_sem=sg_sem.at[t, d],
                recv_sem=rg_sem.at[t, k], device_id={"gx": k}, device_id_type=MESH,
            )

        def along_y(d):
            return pltpu.make_async_remote_copy(
                src_ref=mxs.at[t, 1], dst_ref=mxy.at[t, gy], send_sem=sy_sem.at[t, d],
                recv_sem=ry_sem.at[t, gy], device_id={"gy": lax.rem(gy + d, NY)}, device_id_type=MESH,
            )

        def from_y(d):
            k = lax.rem(gy + d, NY)
            return pltpu.make_async_remote_copy(
                src_ref=mxs.at[t, 1], dst_ref=mxy.at[t, k], send_sem=sy_sem.at[t, d],
                recv_sem=ry_sem.at[t, k], device_id={"gy": k}, device_id_type=MESH,
            )

        for d in range(1, NX):
            along_x(d).start()
        meanwhile()
        for d in range(1, NX):
            from_x(d).wait_recv()
        best = mxg[t, 0]
        for k in range(1, NX):
            best = jnp.maximum(best, mxg[t, k])
        mxs[t, 1] = best
        mxy[t, gy] = best
        for d in range(1, NY):
            along_y(d).start()
        afterwards()
        for d in range(1, NY):
            from_y(d).wait_recv()
        best = mxy[t, 0]
        for k in range(1, NY):
            best = jnp.maximum(best, mxy[t, k])
        for d in range(1, NX):
            along_x(d).wait_send()
        for d in range(1, NY):
            along_y(d).wait_send()
        return best

    for copy in small_copies(0):
        copy.wait()
    mh_r[...] = hz_r[0]
    mh_c[...] = hz_c[0]

    for t in range(ITERS):
        b = t % 2
        last = t == ITERS - 1

        base = []
        mean_now = zmean[...]
        west_halo = [mh_c[0], zero_rows]
        east_halo = [mh_c[1], zero_rows]
        for h in range(2):
            if h == 0:
                pieces = [mh_r[0], mean_now[: 5 * TC]]
            else:
                pieces = [mean_now[3 * TC :], mh_r[1]]
            around = jnp.concatenate(pieces + west_halo + east_halo + [zero_tail], axis=0)
            part = exact_dot(amat[h], around, ((1,), (0,)))
            rows = pl.ds(h * HM, HM)
            base.append((zmean[rows, :] + rates * (part * inv[rows, :])) * links[rows, :])
        base_parts = split(jnp.concatenate(base, axis=0))

        @pl.loop(0, J // 4)
        def _(b):
            kept = source == 4 * b + (place >> 5)
            wide = chars_wide[b] + select_sum(
                base_parts, tuple(kept & (within == 24 + x) for x in range(3))
            )
            here = lane_iota((HM, 128)) >> 5
            for h in range(2):
                for i in range(4):
                    lhs[4 * b + i, h] = jnp.where(
                        here == i, wide[h * HM : (h + 1) * HM], far[i, h]
                    ).astype(BF16)

        share[...] = jnp.zeros((M, 128), F32)

        @pl.loop(0, NC)
        def _(c):
            for copy in edge_copies(t, c, ALL):
                copy.wait_recv()
            den[...] = jnp.ones((M, RC), F32)

            draws_now = draw_rows[:, pl.ds(pl.multiple_of(c * RC, RC), RC)]

            @pl.loop(0, J // 4)
            def _(b4):
                for h in range(2):
                    rows = pl.ds(h * HM, HM)
                    for pair in range(2):
                        q = 2 * b4 + pair
                        sides = jnp.concatenate([hc[t, c, 0, q], hc[t, c, 1, q]], axis=0)
                        total = den[rows, :]
                        for i in (2 * pair, 2 * pair + 1):
                            j = 4 * b4 + i
                            if h == 0:
                                pieces = [hr[t, c, 0, j]] + [st[b, c, j, r] for r in range(5)]
                            else:
                                pieces = [st[b, c, j, r] for r in range(3, 8)] + [hr[t, c, 1, j]]
                            pieces = pieces + [sides]
                            pieces = pieces[: 4 + i] + [draws_now] + pieces[4 + i :]
                            left = jnp.concatenate([near[h], lhs[j, h]], axis=1)
                            summed = lax.dot_general(
                                left, jnp.concatenate(pieces, axis=0), (((1,), (0,)), ((), ())),
                                preferred_element_type=F32,
                            )
                            value = jnp.exp2(summed * gain[rows, :])
                            for part in range(NP):
                                ex[j, part, rows, :] = value[:, part * 128 : (part + 1) * 128]
                            total = total + value
                        den[rows, :] = total

            for part in range(NP):
                rden[part] = 1.0 / den[:, part * 128 : (part + 1) * 128]
            if t == 1:
                for copy in edge_copies(0, c, ALL):
                    copy.wait_send()

            @pl.loop(0, J // 4)
            def _(b4):
                lane = lane_iota((BM, 128))
                for m0 in range(0, M, BM):
                    rows = pl.ds(m0, BM)
                    found = share[rows, :]
                    for i in range(4):
                        j = 4 * b4 + i
                        probs = [ex[j, part, rows, :] * rden[part, rows, :] for part in range(NP)]
                        folded = probs[0]
                        for prob in probs[1:]:
                            folded = folded + prob
                        found = found + jnp.where(lane == j, jnp.sum(folded, axis=1, keepdims=True), 0.0)
                        if not last:
                            for part, prob in enumerate(probs):
                                lanes = pl.ds(part * 128, 128)
                                st[1 - b, c, j, pl.ds(m0 // TC, BM // TC), :, lanes] = (
                                    (prob * spill_ref[j]).astype(BF16).reshape(BM // TC, TC, 128)
                                )
                    share[rows, :] = found
                if not last:
                    for pair in range(2):
                        for side, first in ((0, 0), (1, TC - 1)):
                            at = pl.ds(first, TR, stride=TC)
                            cols = []
                            for j in (4 * b4 + 2 * pair, 4 * b4 + 2 * pair + 1):
                                for part in range(NP):
                                    cols.append(ex[j, part, at, :] * rden[part, at, :] * spill_ref[j])
                            cs[t + 1, c, side, 2 * b4 + pair] = jnp.concatenate(
                                [jnp.concatenate(cols[:NP], axis=1), jnp.concatenate(cols[NP:], axis=1)], axis=0
                            ).astype(BF16)

            if not last:
                @pl.when(c == 0)
                def _():
                    for copy in edge_copies(t + 1, 0, ALL[:1]):
                        copy.start()

        log_share = jnp.log(jnp.where(real, share[...] * (1.0 / R), 1.0))
        residual = jnp.where(real, zobs[...] - log_share, 0.0)
        if not last:
            send_small(t + 1, residual)
        gap = jnp.max(jnp.max(jnp.abs(residual), axis=0, keepdims=True), axis=1, keepdims=True)

        def meanwhile():
            if last:
                for row in range(TR):
                    log_out[:, row, :] = exact_dot(
                        eye_wide, log_share[row * TC : (row + 1) * TC], ((1,), (1,))
                    )

        def afterwards():
            if not last:
                for copy in edge_copies(t + 1, 0, ALL[1:]):
                    copy.start()
                for c in range(1, NC):
                    for copy in edge_copies(t + 1, c, ALL):
                        copy.start()

        best = largest(t, jnp.broadcast_to(gap, (1, 128)), meanwhile, afterwards)
        gap_out[t] = jnp.max(best)
        step = step_level / (best + gap_eps)
        mean_now = zmean[...] + step * residual
        if not last:
            zmean[...] = mean_now
            for copy in small_copies(t + 1):
                copy.wait()
            mh_r[...] = mh_r[...] + step * hz_r[t + 1]
            mh_c[...] = mh_c[...] + step * hz_c[t + 1]
        else:
            for row in range(TR):
                mean_out[:, row, :] = exact_dot(
                    eye_wide, mean_now[row * TC : (row + 1) * TC], ((1,), (1,))
                )

    for e in range(1, ITERS):
        @pl.loop(0, NC)
        def _(c):
            for copy in edge_copies(e, c, ALL):
                copy.wait_send()


def local(*args):
    vmem = pl.BlockSpec(memory_space=pltpu.VMEM)
    smem = pl.BlockSpec(memory_space=pltpu.SMEM)
    anyspace = pl.BlockSpec(memory_space=pl.ANY)
    dma = pltpu.SemaphoreType.DMA
    small = jax.ShapeDtypeStruct((J, TR, TC), F32)
    return pl.pallas_call(
        kernel,
        out_shape=(small, small, jax.ShapeDtypeStruct((ITERS,), F32)),
        in_specs=[vmem, vmem, anyspace, vmem, smem, anyspace, smem, smem, vmem],
        out_specs=(vmem, vmem, smem),
        scratch_shapes=[
            pltpu.VMEM((2, NC, J, TR, TC, RC), BF16),
            pltpu.VMEM((ITERS, NC, 2, J, TC, RC), BF16),
            pltpu.VMEM((ITERS, NC, 2, J // 2, 2 * TR, RC), BF16),
            pltpu.VMEM((ITERS, NC, 2, J // 2, 2 * TR, RC), BF16),
            pltpu.VMEM((J, NP, M, 128), F32),
            pltpu.VMEM((M, RC), F32),
            pltpu.VMEM((NP, M, 128), F32),
            pltpu.VMEM((2, HM, 256), F32),
            pltpu.VMEM((2, HM, 128), BF16),
            pltpu.VMEM((4, 2, HM, 128), F32),
            pltpu.VMEM((J, 2, HM, 128), BF16),
            pltpu.VMEM((J // 4, M, 128), F32),
            pltpu.VMEM((32, R), BF16),
            pltpu.VMEM((4, M, 128), F32),
            pltpu.VMEM((M, 128), F32),
            pltpu.VMEM((M, 128), F32),
            pltpu.VMEM((M, RC), F32),
            pltpu.VMEM((K, J, TR, TC), F32),
            pltpu.VMEM((M, 128), F32),
            pltpu.VMEM((M, 128), F32),
            pltpu.VMEM((ITERS, M, 128), F32),
            pltpu.VMEM((ITERS, 2, TR, 128), F32),
            pltpu.VMEM((ITERS, 2, TC, 128), F32),
            pltpu.VMEM((ITERS, 2, TR, 128), F32),
            pltpu.VMEM((2, TC, 128), F32),
            pltpu.VMEM((2, TR, 128), F32),
            pltpu.VMEM((M, 128), F32),
            pltpu.VMEM((ITERS, 2, 1, 128), F32),
            pltpu.VMEM((ITERS, NX, 1, 128), F32),
            pltpu.VMEM((ITERS, NY, 1, 128), F32),
            dma((NC,)),
            dma,
            dma((ITERS, NC, len(CUTS) - 1, 4)),
            dma((ITERS, NC, len(CUTS) - 1, 4)),
            dma((ITERS, 4)),
            dma((ITERS, 4)),
            dma((ITERS, NX)),
            dma((ITERS, NX)),
            dma((ITERS, NY)),
            dma((ITERS, NY)),
        ],
        compiler_params=pltpu.CompilerParams(
            collective_id=0, has_side_effects=True, vmem_limit_bytes=62 * 1024 * 1024
        ),
    )(*args)


def solution(mesh):
    tile = P(None, "gy", "gx")
    placed = (
        tile, tile, P(None, None, "gy", "gx"), P(), P(), P(None, "gy", "gx", None), P(), P(), tile,
    )
    return jax.shard_map(
        local, mesh=mesh, in_specs=placed, out_specs=(tile, tile, P()), check_vma=False
    )
```

```python
import functools
import math

import jax
import jax.numpy as jnp
from jax import lax
from jax.experimental import pallas as pl
from jax.experimental.pallas import tpu as pltpu
from jax.sharding import PartitionSpec as P

ITERS = 3
J = 32
K = 4
TR = 8
TC = 32
M = TR * TC
HM = M // 2
R = 512
RC = 256
NC = R // RC
NP = RC // 128
NY = 16
NX = 8
BM = 64
CUTS = (0, 16, 20, 32)
ALL = tuple(range(len(CUTS) - 1))
LOG2E = math.log2(math.e)
step_level = 0.2
gap_eps = 1e-06
MESH = pl.DeviceIdType.MESH
F32 = jnp.float32
BF16 = jnp.bfloat16


def lane_iota(shape):
    return lax.broadcasted_iota(jnp.int32, shape, len(shape) - 1)


def row_iota(shape):
    return lax.broadcasted_iota(jnp.int32, shape, len(shape) - 2)


def exact_dot(a, b, dims):
    return lax.dot_general(
        a, b, (dims, ((), ())), precision=lax.Precision.HIGHEST, preferred_element_type=F32
    )


def kernel(
    mean_in, obs_in, chars_in, draws_ref, scale_ref, prior_in, spill_ref, rate_ref, adj_ref,
    mean_out, log_out, gap_out,
    st, hr, hc, cs, ex, den, rden, amat, near, far, lhs, chars_wide, draw_rows, aw, links, inv, gain,
    char_buf, zmean, zobs, zsend, zc_send, hz_r, hz_c, mh_r, mh_c, share, mxs, mxg, mxy,
    prior_sem, char_sem, s_sem, r_sem, sz_sem, rz_sem, sg_sem, rg_sem, sy_sem, ry_sem,
):
    gy = lax.axis_index("gy")
    gx = lax.axis_index("gx")

    def prior_copy(c):
        return pltpu.make_async_copy(
            prior_in.at[:, :, :, pl.ds(pl.multiple_of(c * RC, RC), RC)], st.at[0, c], prior_sem.at[c]
        )

    prior_copy(0).start()
    char_copy = pltpu.make_async_copy(chars_in, char_buf, char_sem)

    barrier = pltpu.get_barrier_semaphore()
    for d in range(1, NX):
        pl.semaphore_signal(
            barrier, inc=1, device_id={"gx": lax.rem(gx + d, NX)}, device_id_type=MESH
        )
    for d in range(1, NY):
        pl.semaphore_signal(
            barrier, inc=1, device_id={"gy": lax.rem(gy + d, NY)}, device_id_type=MESH
        )
    pl.semaphore_wait(barrier, NX - 1 + NY - 1)

    north = {"gy": lax.rem(gy + NY - 1, NY)}
    south = {"gy": lax.rem(gy + 1, NY)}
    west = {"gx": lax.rem(gx + NX - 1, NX)}
    east = {"gx": lax.rem(gx + 1, NX)}

    def edge_copies(e, c, pieces, sides=(0, 1, 2, 3)):
        b = e % 2
        copies = []
        cuts = CUTS if e else (0, J)
        for p in pieces if e else (0,):
            js = pl.ds(cuts[p], cuts[p + 1] - cuts[p])
            qs = pl.ds(cuts[p] // 2, (cuts[p + 1] - cuts[p]) // 2)
            if e:
                last_row, first_row = st.at[b, c, js, TR - 1], st.at[b, c, js, 0]
            else:
                lanes = pl.ds(pl.multiple_of(c * RC, RC), RC)
                last_row, first_row = prior_in.at[:, TR - 1, :, lanes], prior_in.at[:, 0, :, lanes]
            plan = (
                (last_row, hr.at[e, c, 0, js], south),
                (first_row, hr.at[e, c, 1, js], north),
                (cs.at[e, c, 1, qs], hc.at[e, c, 0, qs], east),
                (cs.at[e, c, 0, qs], hc.at[e, c, 1, qs], west),
            )
            for k in sides:
                src, dst, to = plan[k]
                copies.append(
                    pltpu.make_async_remote_copy(
                        src_ref=src, dst_ref=dst, send_sem=s_sem.at[e, c, p, k],
                        recv_sem=r_sem.at[e, c, p, k], device_id=to, device_id_type=MESH,
                    )
                )
        return copies

    def small_copies(x):
        plan = (
            (zsend.at[x, pl.ds(M - TC, TC)], hz_r.at[x, 0], south),
            (zsend.at[x, pl.ds(0, TC)], hz_r.at[x, 1], north),
            (zc_send.at[x, 1], hz_c.at[x, 0], east),
            (zc_send.at[x, 0], hz_c.at[x, 1], west),
        )
        return [
            pltpu.make_async_remote_copy(
                src_ref=src, dst_ref=dst, send_sem=sz_sem.at[x, k], recv_sem=rz_sem.at[x, k],
                device_id=to, device_id_type=MESH,
            )
            for k, (src, dst, to) in enumerate(plan)
        ]

    def send_small(x, value):
        zsend[x] = value
        zc_send[x, 0] = zsend[x, pl.ds(0, TR, stride=TC), :]
        zc_send[x, 1] = zsend[x, pl.ds(TC - 1, TR, stride=TC), :]
        for copy in small_copies(x):
            copy.start()

    for copy in edge_copies(0, 0, ALL, (0, 1)):
        copy.start()
    for c in range(1, NC):
        prior_copy(c).start()
    char_copy.start()

    @pl.loop(0, NC)
    def _(c):
        prior_copy(c).wait()

        @pl.loop(0, J // 2)
        def _(q):
            west_cols = []
            east_cols = []
            for jj in range(2):
                j = 2 * q + jj
                value = st[0, c, j].reshape(M, RC).astype(F32) * spill_ref[j]
                st[0, c, j] = value.astype(BF16).reshape(TR, TC, RC)
                for part in range(NP):
                    ex[j, part] = value[:, part * 128 : (part + 1) * 128]
                for cols, first in ((west_cols, 0), (east_cols, TC - 1)):
                    cols.append(
                        jnp.concatenate(
                            [
                                ex[j, part, pl.ds(first, TR, stride=TC), :]
                                for part in range(NP)
                            ],
                            axis=1,
                        )
                    )
            cs[0, c, 0, q] = jnp.concatenate(west_cols, axis=0).astype(BF16)
            cs[0, c, 1, q] = jnp.concatenate(east_cols, axis=0).astype(BF16)

        for copy in edge_copies(0, c, ALL, (2, 3)):
            copy.start()

        @pl.when(c + 1 < NC)
        def _():
            for copy in edge_copies(0, c + 1, ALL, (0, 1)):
                copy.start()

    eye = (row_iota((TC, TC)) == lane_iota((TC, TC))).astype(F32)
    eye_wide = (row_iota((J, 128)) == lane_iota((J, 128))).astype(F32)
    pad = jnp.zeros((128 - J, TC), F32)

    def to_markets(block):
        return exact_dot(eye, jnp.concatenate([block, pad], axis=0), ((1,), (1,)))

    for row in range(TR):
        rows = pl.ds(row * TC, TC)
        zmean[rows, :] = to_markets(mean_in[:, row, :])
        zobs[rows, :] = to_markets(jnp.log(obs_in[:, row, :]))
    send_small(0, zmean[...])

    for k in range(4):
        for row in range(TR):
            line = adj_ref[k, pl.ds(row, 1), :].astype(F32)
            column = jnp.sum(jnp.where(eye > 0, line, 0.0), axis=1, keepdims=True)
            aw[k, pl.ds(row * TC, TC), :] = jnp.broadcast_to(column, (TC, 128))
    count = jnp.maximum(aw[0] + aw[1] + aw[2] + aw[3], 1.0)
    links[...] = count
    inverse = 1.0 / count
    inv[...] = inverse
    gain[...] = jnp.concatenate([inverse * LOG2E] * (RC // 128), axis=1)

    @pl.loop(0, 2)
    def _(h):
        shape = (HM, 128)
        at = row_iota(shape)
        lane = lane_iota(shape)
        block = lane >> 5
        col = at & (TC - 1)
        row = (at >> 5) + h * (TR // 2)
        mrows = pl.ds(pl.multiple_of(h * HM, HM), HM)
        w0 = jnp.where((row == 0) & (gy == 0), 0.0, aw[0, mrows, :])
        w1 = jnp.where((row == TR - 1) & (gy == NY - 1), 0.0, aw[1, mrows, :])
        w2 = jnp.where((col == 0) & (gx == 0), 0.0, aw[2, mrows, :])
        w3 = jnp.where((col == TC - 1) & (gx == NX - 1), 0.0, aw[3, mrows, :])

        def entries(slot, par):
            west_slot = jnp.where(col == 0, 192 + par * TR + row, at + TC - 1)
            east_slot = jnp.where(col == TC - 1, 208 + par * TR + row, at + TC + 1)
            entry = jnp.where(slot == at, w0, 0.0)
            entry = entry + jnp.where(slot == at + 2 * TC, w1, 0.0)
            entry = entry + jnp.where(slot == west_slot, w2, 0.0)
            return entry + jnp.where(slot == east_slot, w3, 0.0)

        first = entries(lane, 0)
        amat[h, :, pl.ds(0, 128)] = first
        near[h] = first.astype(BF16)
        amat[h, :, pl.ds(128, 128)] = entries(lane + 128, 0)
        for i in range(4):
            slot = jnp.where(block > i, lane + 96, lane + 128)
            far[i, h] = jnp.where(block == i, 0.0, entries(slot, i % 2))

    def split(value):
        high = value.astype(BF16)
        rest = value - high.astype(F32)
        middle = rest.astype(BF16)
        return high, middle, (rest - middle.astype(F32)).astype(BF16)

    def select_sum(parts, masks):
        total = None
        for part, mask in zip(parts, masks):
            term = lax.dot_general(
                part, mask.astype(F32).astype(BF16), (((1,), (0,)), ((), ())), preferred_element_type=F32
            )
            total = term if total is None else total + term
        return total

    char_copy.wait()
    for row in range(TR):
        block = jnp.concatenate([char_buf[k, :, row, :] for k in range(K)], axis=0)
        rows = pl.ds(row * TC, TC)
        ex[0, 0, rows, :] = exact_dot(eye, block, ((1,), (1,))) * links[rows, :]
    char_parts = split(ex[0, 0])
    source = row_iota((128, 128))
    place = lane_iota((128, 128))
    within = place & 31

    @pl.loop(0, J // 4)
    def _(b):
        kept = ((source >> 5) == (within & 3)) & ((source & 31) == 4 * b + (place >> 5))
        term = within >> 2
        chars_wide[b] = select_sum(
            char_parts,
            (
                kept & ((term == 0) | (term == 1) | (term == 4)),
                kept & ((term == 2) | (term == 3)),
                kept & (term == 5),
            ),
        )

    scaled = jnp.concatenate([draws_ref[pl.ds(k, 1), :] * scale_ref[k] for k in range(K)], axis=0)
    high, middle, low = (part.astype(F32) for part in split(scaled))
    draw_rows[...] = jnp.concatenate(
        [high, middle, high, middle, low, high, jnp.ones((3, R), F32), jnp.zeros((5, R), F32)], axis=0
    ).astype(BF16)

    rates = jnp.zeros((1, 128), F32)
    for j in range(J):
        rates = jnp.where(lane_iota((1, 128)) == j, rate_ref[j], rates)
    real = lane_iota((M, 128)) < J
    zero_rows = jnp.zeros((TR, 128), F32)
    zero_tail = jnp.zeros((32, 128), F32)

    def largest(t, value, meanwhile, afterwards):
        mxs[t, 0] = value
        mxg[t, gx] = value

        def along_x(d):
            return pltpu.make_async_remote_copy(
                src_ref=mxs.at[t, 0], dst_ref=mxg.at[t, gx], send_sem=sg_sem.at[t, d],
                recv_sem=rg_sem.at[t, gx], device_id={"gx": lax.rem(gx + d, NX)}, device_id_type=MESH,
            )

        def from_x(d):
            k = lax.rem(gx + d, NX)
            return pltpu.make_async_remote_copy(
                src_ref=mxs.at[t, 0], dst_ref=mxg.at[t, k], send_sem=sg_sem.at[t, d],
                recv_sem=rg_sem.at[t, k], device_id={"gx": k}, device_id_type=MESH,
            )

        def along_y(d):
            return pltpu.make_async_remote_copy(
                src_ref=mxs.at[t, 1], dst_ref=mxy.at[t, gy], send_sem=sy_sem.at[t, d],
                recv_sem=ry_sem.at[t, gy], device_id={"gy": lax.rem(gy + d, NY)}, device_id_type=MESH,
            )

        def from_y(d):
            k = lax.rem(gy + d, NY)
            return pltpu.make_async_remote_copy(
                src_ref=mxs.at[t, 1], dst_ref=mxy.at[t, k], send_sem=sy_sem.at[t, d],
                recv_sem=ry_sem.at[t, k], device_id={"gy": k}, device_id_type=MESH,
            )

        for d in range(1, NX):
            along_x(d).start()
        meanwhile()
        for d in range(1, NX):
            from_x(d).wait_recv()
        best = mxg[t, 0]
        for k in range(1, NX):
            best = jnp.maximum(best, mxg[t, k])
        mxs[t, 1] = best
        mxy[t, gy] = best
        for d in range(1, NY):
            along_y(d).start()
        afterwards()
        for d in range(1, NY):
            from_y(d).wait_recv()
        best = mxy[t, 0]
        for k in range(1, NY):
            best = jnp.maximum(best, mxy[t, k])
        for d in range(1, NX):
            along_x(d).wait_send()
        for d in range(1, NY):
            along_y(d).wait_send()
        return best

    for copy in small_copies(0):
        copy.wait()
    mh_r[...] = hz_r[0]
    mh_c[...] = hz_c[0]

    for t in range(ITERS):
        b = t % 2
        last = t == ITERS - 1

        base = []
        mean_now = zmean[...]
        west_halo = [mh_c[0], zero_rows]
        east_halo = [mh_c[1], zero_rows]
        for h in range(2):
            if h == 0:
                pieces = [mh_r[0], mean_now[: 5 * TC]]
            else:
                pieces = [mean_now[3 * TC :], mh_r[1]]
            around = jnp.concatenate(pieces + west_halo + east_halo + [zero_tail], axis=0)
            part = exact_dot(amat[h], around, ((1,), (0,)))
            rows = pl.ds(h * HM, HM)
            base.append((zmean[rows, :] + rates * (part * inv[rows, :])) * links[rows, :])
        base_parts = split(jnp.concatenate(base, axis=0))

        @pl.loop(0, J // 4)
        def _(b):
            kept = source == 4 * b + (place >> 5)
            wide = chars_wide[b] + select_sum(
                base_parts, tuple(kept & (within == 24 + x) for x in range(3))
            )
            here = lane_iota((HM, 128)) >> 5
            for h in range(2):
                for i in range(4):
                    lhs[4 * b + i, h] = jnp.where(
                        here == i, wide[h * HM : (h + 1) * HM], far[i, h]
                    ).astype(BF16)

        share[...] = jnp.zeros((M, 128), F32)

        @pl.loop(0, NC)
        def _(c):
            for copy in edge_copies(t, c, ALL):
                copy.wait_recv()
            den[...] = jnp.ones((M, RC), F32)

            draws_now = draw_rows[:, pl.ds(pl.multiple_of(c * RC, RC), RC)]

            @pl.loop(0, J // 4)
            def _(b4):
                for h in range(2):
                    rows = pl.ds(h * HM, HM)
                    for pair in range(2):
                        q = 2 * b4 + pair
                        sides = jnp.concatenate([hc[t, c, 0, q], hc[t, c, 1, q]], axis=0)
                        total = den[rows, :]
                        for i in (2 * pair, 2 * pair + 1):
                            j = 4 * b4 + i
                            halo = hr[t, c, h, j]
                            if t == 0:
                                halo = (halo.astype(F32) * spill_ref[j]).astype(BF16)
                            if h == 0:
                                pieces = [halo] + [st[b, c, j, r] for r in range(5)]
                            else:
                                pieces = [st[b, c, j, r] for r in range(3, 8)] + [halo]
                            pieces = pieces + [sides]
                            pieces = pieces[: 4 + i] + [draws_now] + pieces[4 + i :]
                            left = jnp.concatenate([near[h], lhs[j, h]], axis=1)
                            summed = lax.dot_general(
                                left, jnp.concatenate(pieces, axis=0), (((1,), (0,)), ((), ())),
                                preferred_element_type=F32,
                            )
                            value = jnp.exp2(summed * gain[rows, :])
                            for part in range(NP):
                                ex[j, part, rows, :] = value[:, part * 128 : (part + 1) * 128]
                            total = total + value
                        den[rows, :] = total

            for part in range(NP):
                rden[part] = 1.0 / den[:, part * 128 : (part + 1) * 128]
            if t == 1:
                for copy in edge_copies(0, c, ALL):
                    copy.wait_send()

            @pl.loop(0, J // 4)
            def _(b4):
                lane = lane_iota((BM, 128))
                for m0 in range(0, M, BM):
                    rows = pl.ds(m0, BM)
                    found = share[rows, :]
                    for i in range(4):
                        j = 4 * b4 + i
                        probs = [ex[j, part, rows, :] * rden[part, rows, :] for part in range(NP)]
                        folded = probs[0]
                        for prob in probs[1:]:
                            folded = folded + prob
                        found = found + jnp.where(lane == j, jnp.sum(folded, axis=1, keepdims=True), 0.0)
                        if not last:
                            for part, prob in enumerate(probs):
                                lanes = pl.ds(part * 128, 128)
                                st[1 - b, c, j, pl.ds(m0 // TC, BM // TC), :, lanes] = (
                                    (prob * spill_ref[j]).astype(BF16).reshape(BM // TC, TC, 128)
                                )
                    share[rows, :] = found
                if not last:
                    for pair in range(2):
                        for side, first in ((0, 0), (1, TC - 1)):
                            at = pl.ds(first, TR, stride=TC)
                            cols = []
                            for j in (4 * b4 + 2 * pair, 4 * b4 + 2 * pair + 1):
                                for part in range(NP):
                                    cols.append(ex[j, part, at, :] * rden[part, at, :] * spill_ref[j])
                            cs[t + 1, c, side, 2 * b4 + pair] = jnp.concatenate(
                                [jnp.concatenate(cols[:NP], axis=1), jnp.concatenate(cols[NP:], axis=1)], axis=0
                            ).astype(BF16)

            if not last:
                @pl.when(c == 0)
                def _():
                    for copy in edge_copies(t + 1, 0, ALL[:1]):
                        copy.start()

        log_share = jnp.log(jnp.where(real, share[...] * (1.0 / R), 1.0))
        residual = jnp.where(real, zobs[...] - log_share, 0.0)
        if not last:
            send_small(t + 1, residual)
        gap = jnp.max(jnp.max(jnp.abs(residual), axis=0, keepdims=True), axis=1, keepdims=True)

        def meanwhile():
            if not last:
                for copy in edge_copies(t + 1, 0, ALL[1:2]):
                    copy.start()
            if last:
                for row in range(TR):
                    log_out[:, row, :] = exact_dot(
                        eye_wide, log_share[row * TC : (row + 1) * TC], ((1,), (1,))
                    )

        def afterwards():
            if not last:
                for copy in edge_copies(t + 1, 0, ALL[2:]):
                    copy.start()
                for c in range(1, NC):
                    for copy in edge_copies(t + 1, c, ALL):
                        copy.start()

        best = largest(t, jnp.broadcast_to(gap, (1, 128)), meanwhile, afterwards)
        gap_out[t] = jnp.max(best)
        step = step_level / (best + gap_eps)
        mean_now = zmean[...] + step * residual
        if not last:
            zmean[...] = mean_now
            for copy in small_copies(t + 1):
                copy.wait()
            mh_r[...] = mh_r[...] + step * hz_r[t + 1]
            mh_c[...] = mh_c[...] + step * hz_c[t + 1]
        else:
            for row in range(TR):
                mean_out[:, row, :] = exact_dot(
                    eye_wide, mean_now[row * TC : (row + 1) * TC], ((1,), (1,))
                )

    for e in range(1, ITERS):
        @pl.loop(0, NC)
        def _(c):
            for copy in edge_copies(e, c, ALL):
                copy.wait_send()


def put_out(mean_ref, log_ref, gap_ref, mean_out, log_out, gap_out):
    mean_out[...] = mean_ref[...]
    log_out[...] = log_ref[...]
    for t in range(ITERS):
        gap_out[t] = gap_ref[t]


def local(*args):
    vmem = pl.BlockSpec(memory_space=pltpu.VMEM)
    smem = pl.BlockSpec(memory_space=pltpu.SMEM)
    anyspace = pl.BlockSpec(memory_space=pl.ANY)
    dma = pltpu.SemaphoreType.DMA
    small = jax.ShapeDtypeStruct((J, TR, TC), F32)
    out_shape = (small, small, jax.ShapeDtypeStruct((ITERS,), F32))
    found = pl.pallas_call(
        kernel,
        out_shape=out_shape,
        in_specs=[vmem, vmem, anyspace, vmem, smem, anyspace, smem, smem, vmem],
        out_specs=(vmem, vmem, smem),
        scratch_shapes=[
            pltpu.VMEM((2, NC, J, TR, TC, RC), BF16),
            pltpu.VMEM((ITERS, NC, 2, J, TC, RC), BF16),
            pltpu.VMEM((ITERS, NC, 2, J // 2, 2 * TR, RC), BF16),
            pltpu.VMEM((ITERS, NC, 2, J // 2, 2 * TR, RC), BF16),
            pltpu.VMEM((J, NP, M, 128), F32),
            pltpu.VMEM((M, RC), F32),
            pltpu.VMEM((NP, M, 128), F32),
            pltpu.VMEM((2, HM, 256), F32),
            pltpu.VMEM((2, HM, 128), BF16),
            pltpu.VMEM((4, 2, HM, 128), F32),
            pltpu.VMEM((J, 2, HM, 128), BF16),
            pltpu.VMEM((J // 4, M, 128), F32),
            pltpu.VMEM((32, R), BF16),
            pltpu.VMEM((4, M, 128), F32),
            pltpu.VMEM((M, 128), F32),
            pltpu.VMEM((M, 128), F32),
            pltpu.VMEM((M, RC), F32),
            pltpu.VMEM((K, J, TR, TC), F32),
            pltpu.VMEM((M, 128), F32),
            pltpu.VMEM((M, 128), F32),
            pltpu.VMEM((ITERS, M, 128), F32),
            pltpu.VMEM((ITERS, 2, TR, 128), F32),
            pltpu.VMEM((ITERS, 2, TC, 128), F32),
            pltpu.VMEM((ITERS, 2, TR, 128), F32),
            pltpu.VMEM((2, TC, 128), F32),
            pltpu.VMEM((2, TR, 128), F32),
            pltpu.VMEM((M, 128), F32),
            pltpu.VMEM((ITERS, 2, 1, 128), F32),
            pltpu.VMEM((ITERS, NX, 1, 128), F32),
            pltpu.VMEM((ITERS, NY, 1, 128), F32),
            dma((NC,)),
            dma,
            dma((ITERS, NC, len(CUTS) - 1, 4)),
            dma((ITERS, NC, len(CUTS) - 1, 4)),
            dma((ITERS, 4)),
            dma((ITERS, 4)),
            dma((ITERS, NX)),
            dma((ITERS, NX)),
            dma((ITERS, NY)),
            dma((ITERS, NY)),
        ],
        compiler_params=pltpu.CompilerParams(
            collective_id=0, has_side_effects=True, vmem_limit_bytes=62 * 1024 * 1024
        ),
    )(*args)
    return pl.pallas_call(
        put_out, out_shape=out_shape, in_specs=[vmem, vmem, smem], out_specs=(vmem, vmem, smem)
    )(*found)


def solution(mesh):
    tile = P(None, "gy", "gx")
    placed = (
        tile, tile, P(None, None, "gy", "gx"), P(), P(), P(None, "gy", "gx", None), P(), P(), tile,
    )
    return jax.shard_map(
        local, mesh=mesh, in_specs=placed, out_specs=(tile, tile, P()), check_vma=False
    )
```

```python
import functools
import math

import jax
import jax.numpy as jnp
from jax import lax
from jax.experimental import pallas as pl
from jax.experimental.pallas import tpu as pltpu
from jax.sharding import PartitionSpec as P

ITERS = 3
J = 32
K = 4
TR = 8
TC = 32
M = TR * TC
HM = M // 2
R = 512
RC = 256
NC = R // RC
NP = RC // 128
NY = 16
NX = 8
BM = 64
CUTS = (0, 16, 28, 32)
ALL = tuple(range(len(CUTS) - 1))
LOG2E = math.log2(math.e)
step_level = 0.2
gap_eps = 1e-06
MESH = pl.DeviceIdType.MESH
F32 = jnp.float32
BF16 = jnp.bfloat16


def lane_iota(shape):
    return lax.broadcasted_iota(jnp.int32, shape, len(shape) - 1)


def row_iota(shape):
    return lax.broadcasted_iota(jnp.int32, shape, len(shape) - 2)


def exact_dot(a, b, dims):
    return lax.dot_general(
        a, b, (dims, ((), ())), precision=lax.Precision.HIGHEST, preferred_element_type=F32
    )


def kernel(
    mean_in, obs_in, chars_in, draws_ref, scale_ref, prior_in, spill_ref, rate_ref, adj_ref,
    mean_out, log_out, gap_out,
    st, hr, hc, cs, ex, den, rden, amat, near, far, lhs, chars_wide, draw_rows, aw, links, inv, gain,
    char_buf, zmean, zobs, zsend, zc_send, hz_r, hz_c, mh_r, mh_c, share, mxs, mxg, mxy,
    prior_sem, char_sem, s_sem, r_sem, sz_sem, rz_sem, sg_sem, rg_sem, sy_sem, ry_sem,
):
    gy = lax.axis_index("gy")
    gx = lax.axis_index("gx")

    def prior_copy(c):
        return pltpu.make_async_copy(
            prior_in.at[:, :, :, pl.ds(pl.multiple_of(c * RC, RC), RC)], st.at[0, c], prior_sem.at[c]
        )

    prior_copy(0).start()
    char_copy = pltpu.make_async_copy(chars_in, char_buf, char_sem)

    barrier = pltpu.get_barrier_semaphore()
    for d in range(1, NX):
        pl.semaphore_signal(
            barrier, inc=1, device_id={"gx": lax.rem(gx + d, NX)}, device_id_type=MESH
        )
    for d in range(1, NY):
        pl.semaphore_signal(
            barrier, inc=1, device_id={"gy": lax.rem(gy + d, NY)}, device_id_type=MESH
        )
    pl.semaphore_wait(barrier, NX - 1 + NY - 1)

    north = {"gy": lax.rem(gy + NY - 1, NY)}
    south = {"gy": lax.rem(gy + 1, NY)}
    west = {"gx": lax.rem(gx + NX - 1, NX)}
    east = {"gx": lax.rem(gx + 1, NX)}

    def edge_copies(e, c, pieces, sides=(0, 1, 2, 3)):
        b = e % 2
        copies = []
        for p in pieces:
            js = pl.ds(CUTS[p], CUTS[p + 1] - CUTS[p])
            qs = pl.ds(CUTS[p] // 2, (CUTS[p + 1] - CUTS[p]) // 2)
            if e:
                last_row, first_row = st.at[b, c, js, TR - 1], st.at[b, c, js, 0]
            else:
                lanes = pl.ds(pl.multiple_of(c * RC, RC), RC)
                last_row, first_row = prior_in.at[js, TR - 1, :, lanes], prior_in.at[js, 0, :, lanes]
            plan = (
                (last_row, hr.at[e, c, 0, js], south),
                (first_row, hr.at[e, c, 1, js], north),
                (cs.at[e, c, 1, qs], hc.at[e, c, 0, qs], east),
                (cs.at[e, c, 0, qs], hc.at[e, c, 1, qs], west),
            )
            for k in sides:
                src, dst, to = plan[k]
                copies.append(
                    pltpu.make_async_remote_copy(
                        src_ref=src, dst_ref=dst, send_sem=s_sem.at[e, c, p, k],
                        recv_sem=r_sem.at[e, c, p, k], device_id=to, device_id_type=MESH,
                    )
                )
        return copies

    def small_copies(x):
        plan = (
            (zsend.at[x, pl.ds(M - TC, TC)], hz_r.at[x, 0], south),
            (zsend.at[x, pl.ds(0, TC)], hz_r.at[x, 1], north),
            (zc_send.at[x, 1], hz_c.at[x, 0], east),
            (zc_send.at[x, 0], hz_c.at[x, 1], west),
        )
        return [
            pltpu.make_async_remote_copy(
                src_ref=src, dst_ref=dst, send_sem=sz_sem.at[x, k], recv_sem=rz_sem.at[x, k],
                device_id=to, device_id_type=MESH,
            )
            for k, (src, dst, to) in enumerate(plan)
        ]

    def send_small(x, value):
        zsend[x] = value
        zc_send[x, 0] = zsend[x, pl.ds(0, TR, stride=TC), :]
        zc_send[x, 1] = zsend[x, pl.ds(TC - 1, TR, stride=TC), :]
        for copy in small_copies(x):
            copy.start()

    for copy in edge_copies(0, 0, ALL, (0, 1)):
        copy.start()
    for c in range(1, NC):
        prior_copy(c).start()
    char_copy.start()

    @pl.loop(0, NC)
    def _(c):
        prior_copy(c).wait()

        @pl.loop(0, J // 2)
        def _(q):
            west_cols = []
            east_cols = []
            for jj in range(2):
                j = 2 * q + jj
                value = st[0, c, j].reshape(M, RC).astype(F32) * spill_ref[j]
                st[0, c, j] = value.astype(BF16).reshape(TR, TC, RC)
                for part in range(NP):
                    ex[j, part] = value[:, part * 128 : (part + 1) * 128]
                for cols, first in ((west_cols, 0), (east_cols, TC - 1)):
                    cols.append(
                        jnp.concatenate(
                            [
                                ex[j, part, pl.ds(first, TR, stride=TC), :]
                                for part in range(NP)
                            ],
                            axis=1,
                        )
                    )
            cs[0, c, 0, q] = jnp.concatenate(west_cols, axis=0).astype(BF16)
            cs[0, c, 1, q] = jnp.concatenate(east_cols, axis=0).astype(BF16)

        for copy in edge_copies(0, c, ALL, (2, 3)):
            copy.start()

        @pl.when(c + 1 < NC)
        def _():
            for copy in edge_copies(0, c + 1, ALL, (0, 1)):
                copy.start()

    eye = (row_iota((TC, TC)) == lane_iota((TC, TC))).astype(F32)
    eye_wide = (row_iota((J, 128)) == lane_iota((J, 128))).astype(F32)
    pad = jnp.zeros((128 - J, TC), F32)

    def to_markets(block):
        return exact_dot(eye, jnp.concatenate([block, pad], axis=0), ((1,), (1,)))

    for row in range(TR):
        rows = pl.ds(row * TC, TC)
        zmean[rows, :] = to_markets(mean_in[:, row, :])
        zobs[rows, :] = to_markets(jnp.log(obs_in[:, row, :]))
    send_small(0, zmean[...])

    for k in range(4):
        for row in range(TR):
            line = adj_ref[k, pl.ds(row, 1), :].astype(F32)
            column = jnp.sum(jnp.where(eye > 0, line, 0.0), axis=1, keepdims=True)
            aw[k, pl.ds(row * TC, TC), :] = jnp.broadcast_to(column, (TC, 128))
    count = jnp.maximum(aw[0] + aw[1] + aw[2] + aw[3], 1.0)
    links[...] = count
    inverse = 1.0 / count
    inv[...] = inverse
    gain[...] = jnp.concatenate([inverse * LOG2E] * (RC // 128), axis=1)

    @pl.loop(0, 2)
    def _(h):
        shape = (HM, 128)
        at = row_iota(shape)
        lane = lane_iota(shape)
        block = lane >> 5
        col = at & (TC - 1)
        row = (at >> 5) + h * (TR // 2)
        mrows = pl.ds(pl.multiple_of(h * HM, HM), HM)
        w0 = jnp.where((row == 0) & (gy == 0), 0.0, aw[0, mrows, :])
        w1 = jnp.where((row == TR - 1) & (gy == NY - 1), 0.0, aw[1, mrows, :])
        w2 = jnp.where((col == 0) & (gx == 0), 0.0, aw[2, mrows, :])
        w3 = jnp.where((col == TC - 1) & (gx == NX - 1), 0.0, aw[3, mrows, :])

        def entries(slot, par):
            west_slot = jnp.where(col == 0, 192 + par * TR + row, at + TC - 1)
            east_slot = jnp.where(col == TC - 1, 208 + par * TR + row, at + TC + 1)
            entry = jnp.where(slot == at, w0, 0.0)
            entry = entry + jnp.where(slot == at + 2 * TC, w1, 0.0)
            entry = entry + jnp.where(slot == west_slot, w2, 0.0)
            return entry + jnp.where(slot == east_slot, w3, 0.0)

        first = entries(lane, 0)
        amat[h, :, pl.ds(0, 128)] = first
        near[h] = first.astype(BF16)
        amat[h, :, pl.ds(128, 128)] = entries(lane + 128, 0)
        for i in range(4):
            slot = jnp.where(block > i, lane + 96, lane + 128)
            far[i, h] = jnp.where(block == i, 0.0, entries(slot, i % 2))

    def split(value):
        high = value.astype(BF16)
        rest = value - high.astype(F32)
        middle = rest.astype(BF16)
        return high, middle, (rest - middle.astype(F32)).astype(BF16)

    def select_sum(parts, masks):
        total = None
        for part, mask in zip(parts, masks):
            term = lax.dot_general(
                part, mask.astype(F32).astype(BF16), (((1,), (0,)), ((), ())), preferred_element_type=F32
            )
            total = term if total is None else total + term
        return total

    char_copy.wait()
    for row in range(TR):
        block = jnp.concatenate([char_buf[k, :, row, :] for k in range(K)], axis=0)
        rows = pl.ds(row * TC, TC)
        ex[0, 0, rows, :] = exact_dot(eye, block, ((1,), (1,))) * links[rows, :]
    char_parts = split(ex[0, 0])
    source = row_iota((128, 128))
    place = lane_iota((128, 128))
    within = place & 31

    @pl.loop(0, J // 4)
    def _(b):
        kept = ((source >> 5) == (within & 3)) & ((source & 31) == 4 * b + (place >> 5))
        term = within >> 2
        chars_wide[b] = select_sum(
            char_parts,
            (
                kept & ((term == 0) | (term == 1) | (term == 4)),
                kept & ((term == 2) | (term == 3)),
                kept & (term == 5),
            ),
        )

    scaled = jnp.concatenate([draws_ref[pl.ds(k, 1), :] * scale_ref[k] for k in range(K)], axis=0)
    high, middle, low = (part.astype(F32) for part in split(scaled))
    draw_rows[...] = jnp.concatenate(
        [high, middle, high, middle, low, high, jnp.ones((3, R), F32), jnp.zeros((5, R), F32)], axis=0
    ).astype(BF16)

    rates = jnp.zeros((1, 128), F32)
    for j in range(J):
        rates = jnp.where(lane_iota((1, 128)) == j, rate_ref[j], rates)
    real = lane_iota((M, 128)) < J
    zero_rows = jnp.zeros((TR, 128), F32)
    zero_tail = jnp.zeros((32, 128), F32)

    def largest(t, value, meanwhile, afterwards):
        mxs[t, 0] = value
        mxg[t, gx] = value

        def along_x(d):
            return pltpu.make_async_remote_copy(
                src_ref=mxs.at[t, 0], dst_ref=mxg.at[t, gx], send_sem=sg_sem.at[t, d],
                recv_sem=rg_sem.at[t, gx], device_id={"gx": lax.rem(gx + d, NX)}, device_id_type=MESH,
            )

        def from_x(d):
            k = lax.rem(gx + d, NX)
            return pltpu.make_async_remote_copy(
                src_ref=mxs.at[t, 0], dst_ref=mxg.at[t, k], send_sem=sg_sem.at[t, d],
                recv_sem=rg_sem.at[t, k], device_id={"gx": k}, device_id_type=MESH,
            )

        def along_y(d):
            return pltpu.make_async_remote_copy(
                src_ref=mxs.at[t, 1], dst_ref=mxy.at[t, gy], send_sem=sy_sem.at[t, d],
                recv_sem=ry_sem.at[t, gy], device_id={"gy": lax.rem(gy + d, NY)}, device_id_type=MESH,
            )

        def from_y(d):
            k = lax.rem(gy + d, NY)
            return pltpu.make_async_remote_copy(
                src_ref=mxs.at[t, 1], dst_ref=mxy.at[t, k], send_sem=sy_sem.at[t, d],
                recv_sem=ry_sem.at[t, k], device_id={"gy": k}, device_id_type=MESH,
            )

        for d in range(1, NX):
            along_x(d).start()
        meanwhile()
        for d in range(1, NX):
            from_x(d).wait_recv()
        best = mxg[t, 0]
        for k in range(1, NX):
            best = jnp.maximum(best, mxg[t, k])
        mxs[t, 1] = best
        mxy[t, gy] = best
        for d in range(1, NY):
            along_y(d).start()
        afterwards()
        for d in range(1, NY):
            from_y(d).wait_recv()
        best = mxy[t, 0]
        for k in range(1, NY):
            best = jnp.maximum(best, mxy[t, k])
        for d in range(1, NX):
            along_x(d).wait_send()
        for d in range(1, NY):
            along_y(d).wait_send()
        return best

    for copy in small_copies(0):
        copy.wait()
    mh_r[...] = hz_r[0]
    mh_c[...] = hz_c[0]

    for t in range(ITERS):
        b = t % 2
        last = t == ITERS - 1

        base = []
        mean_now = zmean[...]
        west_halo = [mh_c[0], zero_rows]
        east_halo = [mh_c[1], zero_rows]
        for h in range(2):
            if h == 0:
                pieces = [mh_r[0], mean_now[: 5 * TC]]
            else:
                pieces = [mean_now[3 * TC :], mh_r[1]]
            around = jnp.concatenate(pieces + west_halo + east_halo + [zero_tail], axis=0)
            part = exact_dot(amat[h], around, ((1,), (0,)))
            rows = pl.ds(h * HM, HM)
            base.append((zmean[rows, :] + rates * (part * inv[rows, :])) * links[rows, :])
        base_parts = split(jnp.concatenate(base, axis=0))

        @pl.loop(0, J // 4)
        def _(b):
            kept = source == 4 * b + (place >> 5)
            wide = chars_wide[b] + select_sum(
                base_parts, tuple(kept & (within == 24 + x) for x in range(3))
            )
            here = lane_iota((HM, 128)) >> 5
            for h in range(2):
                for i in range(4):
                    lhs[4 * b + i, h] = jnp.where(
                        here == i, wide[h * HM : (h + 1) * HM], far[i, h]
                    ).astype(BF16)

        share[...] = jnp.zeros((M, 128), F32)

        @pl.loop(0, NC)
        def _(c):
            den[...] = jnp.ones((M, RC), F32)

            draws_now = draw_rows[:, pl.ds(pl.multiple_of(c * RC, RC), RC)]

            @pl.loop(0, J // 4)
            def _(b4):
                for p in ALL:
                    @pl.when(b4 == CUTS[p] // 4)
                    def _(p=p):
                        for copy in edge_copies(t, c, (p,)):
                            copy.wait_recv()

                for h in range(2):
                    rows = pl.ds(h * HM, HM)
                    for pair in range(2):
                        q = 2 * b4 + pair
                        sides = jnp.concatenate([hc[t, c, 0, q], hc[t, c, 1, q]], axis=0)
                        total = den[rows, :]
                        for i in (2 * pair, 2 * pair + 1):
                            j = 4 * b4 + i
                            halo = hr[t, c, h, j]
                            if t == 0:
                                halo = (halo.astype(F32) * spill_ref[j]).astype(BF16)
                            if h == 0:
                                pieces = [halo] + [st[b, c, j, r] for r in range(5)]
                            else:
                                pieces = [st[b, c, j, r] for r in range(3, 8)] + [halo]
                            pieces = pieces + [sides]
                            pieces = pieces[: 4 + i] + [draws_now] + pieces[4 + i :]
                            left = jnp.concatenate([near[h], lhs[j, h]], axis=1)
                            summed = lax.dot_general(
                                left, jnp.concatenate(pieces, axis=0), (((1,), (0,)), ((), ())),
                                preferred_element_type=F32,
                            )
                            value = jnp.exp2(summed * gain[rows, :])
                            for part in range(NP):
                                ex[j, part, rows, :] = value[:, part * 128 : (part + 1) * 128]
                            total = total + value
                        den[rows, :] = total

            for part in range(NP):
                rden[part] = 1.0 / den[:, part * 128 : (part + 1) * 128]
            if t == 1:
                for copy in edge_copies(0, c, ALL):
                    copy.wait_send()

            @pl.loop(0, J // 4)
            def _(b4):
                lane = lane_iota((BM, 128))
                for m0 in range(0, M, BM):
                    rows = pl.ds(m0, BM)
                    found = share[rows, :]
                    for i in range(4):
                        j = 4 * b4 + i
                        probs = [ex[j, part, rows, :] * rden[part, rows, :] for part in range(NP)]
                        folded = probs[0]
                        for prob in probs[1:]:
                            folded = folded + prob
                        found = found + jnp.where(lane == j, jnp.sum(folded, axis=1, keepdims=True), 0.0)
                        if not last:
                            for part, prob in enumerate(probs):
                                lanes = pl.ds(part * 128, 128)
                                st[1 - b, c, j, pl.ds(m0 // TC, BM // TC), :, lanes] = (
                                    (prob * spill_ref[j]).astype(BF16).reshape(BM // TC, TC, 128)
                                )
                    share[rows, :] = found
                if not last:
                    for pair in range(2):
                        for side, first in ((0, 0), (1, TC - 1)):
                            at = pl.ds(first, TR, stride=TC)
                            cols = []
                            for j in (4 * b4 + 2 * pair, 4 * b4 + 2 * pair + 1):
                                for part in range(NP):
                                    cols.append(ex[j, part, at, :] * rden[part, at, :] * spill_ref[j])
                            cs[t + 1, c, side, 2 * b4 + pair] = jnp.concatenate(
                                [jnp.concatenate(cols[:NP], axis=1), jnp.concatenate(cols[NP:], axis=1)], axis=0
                            ).astype(BF16)

            if not last:
                @pl.when(c == 0)
                def _():
                    for copy in edge_copies(t + 1, 0, ALL[:1]):
                        copy.start()

        log_share = jnp.log(jnp.where(real, share[...] * (1.0 / R), 1.0))
        residual = jnp.where(real, zobs[...] - log_share, 0.0)
        if not last:
            send_small(t + 1, residual)
        gap = jnp.max(jnp.max(jnp.abs(residual), axis=0, keepdims=True), axis=1, keepdims=True)

        def meanwhile():
            if not last:
                for copy in edge_copies(t + 1, 0, ALL[1:2]):
                    copy.start()
            if last:
                for row in range(TR):
                    log_out[:, row, :] = exact_dot(
                        eye_wide, log_share[row * TC : (row + 1) * TC], ((1,), (1,))
                    )

        def afterwards():
            if not last:
                for copy in edge_copies(t + 1, 0, ALL[2:]):
                    copy.start()
                for c in range(1, NC):
                    for copy in edge_copies(t + 1, c, ALL):
                        copy.start()

        best = largest(t, jnp.broadcast_to(gap, (1, 128)), meanwhile, afterwards)
        gap_out[t] = jnp.max(best)
        step = step_level / (best + gap_eps)
        mean_now = zmean[...] + step * residual
        if not last:
            zmean[...] = mean_now
            for copy in small_copies(t + 1):
                copy.wait()
            mh_r[...] = mh_r[...] + step * hz_r[t + 1]
            mh_c[...] = mh_c[...] + step * hz_c[t + 1]
        else:
            for row in range(TR):
                mean_out[:, row, :] = exact_dot(
                    eye_wide, mean_now[row * TC : (row + 1) * TC], ((1,), (1,))
                )

    for e in range(1, ITERS):
        @pl.loop(0, NC)
        def _(c):
            for copy in edge_copies(e, c, ALL):
                copy.wait_send()


def put_out(mean_ref, log_ref, gap_ref, mean_out, log_out, gap_out):
    mean_out[...] = mean_ref[...]
    log_out[...] = log_ref[...]
    for t in range(ITERS):
        gap_out[t] = gap_ref[t]


def local(*args):
    vmem = pl.BlockSpec(memory_space=pltpu.VMEM)
    smem = pl.BlockSpec(memory_space=pltpu.SMEM)
    anyspace = pl.BlockSpec(memory_space=pl.ANY)
    dma = pltpu.SemaphoreType.DMA
    small = jax.ShapeDtypeStruct((J, TR, TC), F32)
    out_shape = (small, small, jax.ShapeDtypeStruct((ITERS,), F32))
    found = pl.pallas_call(
        kernel,
        out_shape=out_shape,
        in_specs=[vmem, vmem, anyspace, vmem, smem, anyspace, smem, smem, vmem],
        out_specs=(vmem, vmem, smem),
        scratch_shapes=[
            pltpu.VMEM((2, NC, J, TR, TC, RC), BF16),
            pltpu.VMEM((ITERS, NC, 2, J, TC, RC), BF16),
            pltpu.VMEM((ITERS, NC, 2, J // 2, 2 * TR, RC), BF16),
            pltpu.VMEM((ITERS, NC, 2, J // 2, 2 * TR, RC), BF16),
            pltpu.VMEM((J, NP, M, 128), F32),
            pltpu.VMEM((M, RC), F32),
            pltpu.VMEM((NP, M, 128), F32),
            pltpu.VMEM((2, HM, 256), F32),
            pltpu.VMEM((2, HM, 128), BF16),
            pltpu.VMEM((4, 2, HM, 128), F32),
            pltpu.VMEM((J, 2, HM, 128), BF16),
            pltpu.VMEM((J // 4, M, 128), F32),
            pltpu.VMEM((32, R), BF16),
            pltpu.VMEM((4, M, 128), F32),
            pltpu.VMEM((M, 128), F32),
            pltpu.VMEM((M, 128), F32),
            pltpu.VMEM((M, RC), F32),
            pltpu.VMEM((K, J, TR, TC), F32),
            pltpu.VMEM((M, 128), F32),
            pltpu.VMEM((M, 128), F32),
            pltpu.VMEM((ITERS, M, 128), F32),
            pltpu.VMEM((ITERS, 2, TR, 128), F32),
            pltpu.VMEM((ITERS, 2, TC, 128), F32),
            pltpu.VMEM((ITERS, 2, TR, 128), F32),
            pltpu.VMEM((2, TC, 128), F32),
            pltpu.VMEM((2, TR, 128), F32),
            pltpu.VMEM((M, 128), F32),
            pltpu.VMEM((ITERS, 2, 1, 128), F32),
            pltpu.VMEM((ITERS, NX, 1, 128), F32),
            pltpu.VMEM((ITERS, NY, 1, 128), F32),
            dma((NC,)),
            dma,
            dma((ITERS, NC, len(CUTS) - 1, 4)),
            dma((ITERS, NC, len(CUTS) - 1, 4)),
            dma((ITERS, 4)),
            dma((ITERS, 4)),
            dma((ITERS, NX)),
            dma((ITERS, NX)),
            dma((ITERS, NY)),
            dma((ITERS, NY)),
        ],
        compiler_params=pltpu.CompilerParams(
            collective_id=0, has_side_effects=True, vmem_limit_bytes=62 * 1024 * 1024
        ),
    )(*args)
    return pl.pallas_call(
        put_out, out_shape=out_shape, in_specs=[vmem, vmem, smem], out_specs=(vmem, vmem, smem)
    )(*found)


def solution(mesh):
    tile = P(None, "gy", "gx")
    placed = (
        tile, tile, P(None, None, "gy", "gx"), P(), P(), P(None, "gy", "gx", None), P(), P(), tile,
    )
    return jax.shard_map(
        local, mesh=mesh, in_specs=placed, out_specs=(tile, tile, P()), check_vma=False
    )
```

```python
import functools
import math

import jax
import jax.numpy as jnp
from jax import lax
from jax.experimental import pallas as pl
from jax.experimental.pallas import tpu as pltpu
from jax.sharding import PartitionSpec as P

ITERS = 3
J = 32
K = 4
TR = 8
TC = 32
M = TR * TC
HM = M // 2
R = 512
RC = 256
NC = R // RC
NP = RC // 128
NY = 16
NX = 8
BM = 64
CUTS = (0, 16, 28, 32)
ALL = tuple(range(len(CUTS) - 1))
LOG2E = math.log2(math.e)
step_level = 0.2
gap_eps = 1e-06
MESH = pl.DeviceIdType.MESH
F32 = jnp.float32
BF16 = jnp.bfloat16


def lane_iota(shape):
    return lax.broadcasted_iota(jnp.int32, shape, len(shape) - 1)


def row_iota(shape):
    return lax.broadcasted_iota(jnp.int32, shape, len(shape) - 2)


def exact_dot(a, b, dims):
    return lax.dot_general(
        a, b, (dims, ((), ())), precision=lax.Precision.HIGHEST, preferred_element_type=F32
    )


def kernel(
    mean_hbm, obs_hbm, chars_in, draws_hbm, scale_ref, prior_in, spill_ref, rate_ref, adj_hbm,
    mean_out, log_out, gap_out,
    st, hr, hc, cs, ex, den, rden, amat, near, far, lhs, chars_wide, draw_rows, aw, links, inv, gain,
    char_buf, mean_in, obs_in, draws_ref, adj_ref, small_sem, zmean, zobs, zsend, zc_send, hz_r, hz_c, mh_r, mh_c, share, mxs, mxg, mxy,
    prior_sem, char_sem, s_sem, r_sem, sz_sem, rz_sem, sg_sem, rg_sem, sy_sem, ry_sem,
):
    gy = lax.axis_index("gy")
    gx = lax.axis_index("gx")

    def prior_copy(c):
        return pltpu.make_async_copy(
            prior_in.at[:, :, :, pl.ds(pl.multiple_of(c * RC, RC), RC)], st.at[0, c], prior_sem.at[c]
        )

    prior_copy(0).start()
    char_copy = pltpu.make_async_copy(chars_in, char_buf, char_sem)

    barrier = pltpu.get_barrier_semaphore()
    for d in range(1, NX):
        pl.semaphore_signal(
            barrier, inc=1, device_id={"gx": lax.rem(gx + d, NX)}, device_id_type=MESH
        )
    for d in range(1, NY):
        pl.semaphore_signal(
            barrier, inc=1, device_id={"gy": lax.rem(gy + d, NY)}, device_id_type=MESH
        )
    pl.semaphore_wait(barrier, NX - 1 + NY - 1)

    north = {"gy": lax.rem(gy + NY - 1, NY)}
    south = {"gy": lax.rem(gy + 1, NY)}
    west = {"gx": lax.rem(gx + NX - 1, NX)}
    east = {"gx": lax.rem(gx + 1, NX)}

    def edge_copies(e, c, pieces, sides=(0, 1, 2, 3)):
        b = e % 2
        copies = []
        for p in pieces:
            js = pl.ds(CUTS[p], CUTS[p + 1] - CUTS[p])
            qs = pl.ds(CUTS[p] // 2, (CUTS[p + 1] - CUTS[p]) // 2)
            if e:
                last_row, first_row = st.at[b, c, js, TR - 1], st.at[b, c, js, 0]
            else:
                lanes = pl.ds(pl.multiple_of(c * RC, RC), RC)
                last_row, first_row = prior_in.at[js, TR - 1, :, lanes], prior_in.at[js, 0, :, lanes]
            plan = (
                (last_row, hr.at[e, c, 0, js], south),
                (first_row, hr.at[e, c, 1, js], north),
                (cs.at[e, c, 1, qs], hc.at[e, c, 0, qs], east),
                (cs.at[e, c, 0, qs], hc.at[e, c, 1, qs], west),
            )
            for k in sides:
                src, dst, to = plan[k]
                copies.append(
                    pltpu.make_async_remote_copy(
                        src_ref=src, dst_ref=dst, send_sem=s_sem.at[e, c, p, k],
                        recv_sem=r_sem.at[e, c, p, k], device_id=to, device_id_type=MESH,
                    )
                )
        return copies

    def small_copies(x):
        plan = (
            (zsend.at[x, pl.ds(M - TC, TC)], hz_r.at[x, 0], south),
            (zsend.at[x, pl.ds(0, TC)], hz_r.at[x, 1], north),
            (zc_send.at[x, 1], hz_c.at[x, 0], east),
            (zc_send.at[x, 0], hz_c.at[x, 1], west),
        )
        return [
            pltpu.make_async_remote_copy(
                src_ref=src, dst_ref=dst, send_sem=sz_sem.at[x, k], recv_sem=rz_sem.at[x, k],
                device_id=to, device_id_type=MESH,
            )
            for k, (src, dst, to) in enumerate(plan)
        ]

    def send_small(x, value):
        zsend[x] = value
        zc_send[x, 0] = zsend[x, pl.ds(0, TR, stride=TC), :]
        zc_send[x, 1] = zsend[x, pl.ds(TC - 1, TR, stride=TC), :]
        for copy in small_copies(x):
            copy.start()

    for copy in edge_copies(0, 0, ALL, (0, 1)):
        copy.start()
    for c in range(1, NC):
        prior_copy(c).start()
    char_copy.start()
    inputs = [
        pltpu.make_async_copy(src, dst, small_sem.at[k])
        for k, (src, dst) in enumerate(
            ((mean_hbm, mean_in), (obs_hbm, obs_in), (draws_hbm, draws_ref), (adj_hbm, adj_ref))
        )
    ]
    for copy in inputs:
        copy.start()

    @pl.loop(0, NC)
    def _(c):
        prior_copy(c).wait()

        @pl.loop(0, J // 2)
        def _(q):
            west_cols = []
            east_cols = []
            for jj in range(2):
                j = 2 * q + jj
                value = st[0, c, j].reshape(M, RC).astype(F32) * spill_ref[j]
                st[0, c, j] = value.astype(BF16).reshape(TR, TC, RC)
                for part in range(NP):
                    ex[j, part] = value[:, part * 128 : (part + 1) * 128]
                for cols, first in ((west_cols, 0), (east_cols, TC - 1)):
                    cols.append(
                        jnp.concatenate(
                            [
                                ex[j, part, pl.ds(first, TR, stride=TC), :]
                                for part in range(NP)
                            ],
                            axis=1,
                        )
                    )
            cs[0, c, 0, q] = jnp.concatenate(west_cols, axis=0).astype(BF16)
            cs[0, c, 1, q] = jnp.concatenate(east_cols, axis=0).astype(BF16)

        for copy in edge_copies(0, c, ALL, (2, 3)):
            copy.start()

        @pl.when(c + 1 < NC)
        def _():
            for copy in edge_copies(0, c + 1, ALL, (0, 1)):
                copy.start()

    for copy in inputs:
        copy.wait()

    eye = (row_iota((TC, TC)) == lane_iota((TC, TC))).astype(F32)
    eye_wide = (row_iota((J, 128)) == lane_iota((J, 128))).astype(F32)
    pad = jnp.zeros((128 - J, TC), F32)

    def to_markets(block):
        return exact_dot(eye, jnp.concatenate([block, pad], axis=0), ((1,), (1,)))

    for row in range(TR):
        rows = pl.ds(row * TC, TC)
        zmean[rows, :] = to_markets(mean_in[:, row, :])
        zobs[rows, :] = to_markets(jnp.log(obs_in[:, row, :]))
    send_small(0, zmean[...])

    for k in range(4):
        for row in range(TR):
            line = adj_ref[k, pl.ds(row, 1), :].astype(F32)
            column = jnp.sum(jnp.where(eye > 0, line, 0.0), axis=1, keepdims=True)
            aw[k, pl.ds(row * TC, TC), :] = jnp.broadcast_to(column, (TC, 128))
    count = jnp.maximum(aw[0] + aw[1] + aw[2] + aw[3], 1.0)
    links[...] = count
    inverse = 1.0 / count
    inv[...] = inverse
    gain[...] = jnp.concatenate([inverse * LOG2E] * (RC // 128), axis=1)

    @pl.loop(0, 2)
    def _(h):
        shape = (HM, 128)
        at = row_iota(shape)
        lane = lane_iota(shape)
        block = lane >> 5
        col = at & (TC - 1)
        row = (at >> 5) + h * (TR // 2)
        mrows = pl.ds(pl.multiple_of(h * HM, HM), HM)
        w0 = jnp.where((row == 0) & (gy == 0), 0.0, aw[0, mrows, :])
        w1 = jnp.where((row == TR - 1) & (gy == NY - 1), 0.0, aw[1, mrows, :])
        w2 = jnp.where((col == 0) & (gx == 0), 0.0, aw[2, mrows, :])
        w3 = jnp.where((col == TC - 1) & (gx == NX - 1), 0.0, aw[3, mrows, :])

        def entries(slot, par):
            west_slot = jnp.where(col == 0, 192 + par * TR + row, at + TC - 1)
            east_slot = jnp.where(col == TC - 1, 208 + par * TR + row, at + TC + 1)
            entry = jnp.where(slot == at, w0, 0.0)
            entry = entry + jnp.where(slot == at + 2 * TC, w1, 0.0)
            entry = entry + jnp.where(slot == west_slot, w2, 0.0)
            return entry + jnp.where(slot == east_slot, w3, 0.0)

        first = entries(lane, 0)
        amat[h, :, pl.ds(0, 128)] = first
        near[h] = first.astype(BF16)
        amat[h, :, pl.ds(128, 128)] = entries(lane + 128, 0)
        for i in range(4):
            slot = jnp.where(block > i, lane + 96, lane + 128)
            far[i, h] = jnp.where(block == i, 0.0, entries(slot, i % 2))

    def split(value):
        high = value.astype(BF16)
        rest = value - high.astype(F32)
        middle = rest.astype(BF16)
        return high, middle, (rest - middle.astype(F32)).astype(BF16)

    def select_sum(parts, masks):
        total = None
        for part, mask in zip(parts, masks):
            term = lax.dot_general(
                part, mask.astype(F32).astype(BF16), (((1,), (0,)), ((), ())), preferred_element_type=F32
            )
            total = term if total is None else total + term
        return total

    char_copy.wait()
    for row in range(TR):
        block = jnp.concatenate([char_buf[k, :, row, :] for k in range(K)], axis=0)
        rows = pl.ds(row * TC, TC)
        ex[0, 0, rows, :] = exact_dot(eye, block, ((1,), (1,))) * links[rows, :]
    char_parts = split(ex[0, 0])
    source = row_iota((128, 128))
    place = lane_iota((128, 128))
    within = place & 31

    @pl.loop(0, J // 4)
    def _(b):
        kept = ((source >> 5) == (within & 3)) & ((source & 31) == 4 * b + (place >> 5))
        term = within >> 2
        chars_wide[b] = select_sum(
            char_parts,
            (
                kept & ((term == 0) | (term == 1) | (term == 4)),
                kept & ((term == 2) | (term == 3)),
                kept & (term == 5),
            ),
        )

    scaled = jnp.concatenate([draws_ref[pl.ds(k, 1), :] * scale_ref[k] for k in range(K)], axis=0)
    high, middle, low = (part.astype(F32) for part in split(scaled))
    draw_rows[...] = jnp.concatenate(
        [high, middle, high, middle, low, high, jnp.ones((3, R), F32), jnp.zeros((5, R), F32)], axis=0
    ).astype(BF16)

    rates = jnp.zeros((1, 128), F32)
    for j in range(J):
        rates = jnp.where(lane_iota((1, 128)) == j, rate_ref[j], rates)
    real = lane_iota((M, 128)) < J
    zero_rows = jnp.zeros((TR, 128), F32)
    zero_tail = jnp.zeros((32, 128), F32)

    def largest(t, value, meanwhile, afterwards):
        mxs[t, 0] = value
        mxg[t, gx] = value

        def along_x(d):
            return pltpu.make_async_remote_copy(
                src_ref=mxs.at[t, 0], dst_ref=mxg.at[t, gx], send_sem=sg_sem.at[t, d],
                recv_sem=rg_sem.at[t, gx], device_id={"gx": lax.rem(gx + d, NX)}, device_id_type=MESH,
            )

        def from_x(d):
            k = lax.rem(gx + d, NX)
            return pltpu.make_async_remote_copy(
                src_ref=mxs.at[t, 0], dst_ref=mxg.at[t, k], send_sem=sg_sem.at[t, d],
                recv_sem=rg_sem.at[t, k], device_id={"gx": k}, device_id_type=MESH,
            )

        def along_y(d):
            return pltpu.make_async_remote_copy(
                src_ref=mxs.at[t, 1], dst_ref=mxy.at[t, gy], send_sem=sy_sem.at[t, d],
                recv_sem=ry_sem.at[t, gy], device_id={"gy": lax.rem(gy + d, NY)}, device_id_type=MESH,
            )

        def from_y(d):
            k = lax.rem(gy + d, NY)
            return pltpu.make_async_remote_copy(
                src_ref=mxs.at[t, 1], dst_ref=mxy.at[t, k], send_sem=sy_sem.at[t, d],
                recv_sem=ry_sem.at[t, k], device_id={"gy": k}, device_id_type=MESH,
            )

        for d in range(1, NX):
            along_x(d).start()
        meanwhile()
        for d in range(1, NX):
            from_x(d).wait_recv()
        best = mxg[t, 0]
        for k in range(1, NX):
            best = jnp.maximum(best, mxg[t, k])
        mxs[t, 1] = best
        mxy[t, gy] = best
        for d in range(1, NY):
            along_y(d).start()
        afterwards()
        for d in range(1, NY):
            from_y(d).wait_recv()
        best = mxy[t, 0]
        for k in range(1, NY):
            best = jnp.maximum(best, mxy[t, k])
        return best

    for copy in small_copies(0):
        copy.wait()
    mh_r[...] = hz_r[0]
    mh_c[...] = hz_c[0]

    for t in range(ITERS):
        b = t % 2
        last = t == ITERS - 1

        base = []
        mean_now = zmean[...]
        west_halo = [mh_c[0], zero_rows]
        east_halo = [mh_c[1], zero_rows]
        for h in range(2):
            if h == 0:
                pieces = [mh_r[0], mean_now[: 5 * TC]]
            else:
                pieces = [mean_now[3 * TC :], mh_r[1]]
            around = jnp.concatenate(pieces + west_halo + east_halo + [zero_tail], axis=0)
            part = exact_dot(amat[h], around, ((1,), (0,)))
            rows = pl.ds(h * HM, HM)
            base.append((zmean[rows, :] + rates * (part * inv[rows, :])) * links[rows, :])
        base_parts = split(jnp.concatenate(base, axis=0))

        @pl.loop(0, J // 4)
        def _(b):
            kept = source == 4 * b + (place >> 5)
            wide = chars_wide[b] + select_sum(
                base_parts, tuple(kept & (within == 24 + x) for x in range(3))
            )
            here = lane_iota((HM, 128)) >> 5
            for h in range(2):
                for i in range(4):
                    lhs[4 * b + i, h] = jnp.where(
                        here == i, wide[h * HM : (h + 1) * HM], far[i, h]
                    ).astype(BF16)

        share[...] = jnp.zeros((M, 128), F32)

        @pl.loop(0, NC)
        def _(c):
            den[...] = jnp.ones((M, RC), F32)

            draws_now = draw_rows[:, pl.ds(pl.multiple_of(c * RC, RC), RC)]

            @pl.loop(0, J // 4)
            def _(b4):
                for p in ALL:
                    @pl.when(b4 == CUTS[p] // 4)
                    def _(p=p):
                        for copy in edge_copies(t, c, (p,)):
                            copy.wait_recv()

                for h in range(2):
                    rows = pl.ds(h * HM, HM)
                    for pair in range(2):
                        q = 2 * b4 + pair
                        sides = jnp.concatenate([hc[t, c, 0, q], hc[t, c, 1, q]], axis=0)
                        total = den[rows, :]
                        for i in (2 * pair, 2 * pair + 1):
                            j = 4 * b4 + i
                            halo = hr[t, c, h, j]
                            if t == 0:
                                halo = (halo.astype(F32) * spill_ref[j]).astype(BF16)
                            if h == 0:
                                pieces = [halo] + [st[b, c, j, r] for r in range(5)]
                            else:
                                pieces = [st[b, c, j, r] for r in range(3, 8)] + [halo]
                            pieces = pieces + [sides]
                            pieces = pieces[: 4 + i] + [draws_now] + pieces[4 + i :]
                            left = jnp.concatenate([near[h], lhs[j, h]], axis=1)
                            summed = lax.dot_general(
                                left, jnp.concatenate(pieces, axis=0), (((1,), (0,)), ((), ())),
                                preferred_element_type=F32,
                            )
                            value = jnp.exp2(summed * gain[rows, :])
                            for part in range(NP):
                                ex[j, part, rows, :] = value[:, part * 128 : (part + 1) * 128]
                            total = total + value
                        den[rows, :] = total

            for part in range(NP):
                rden[part] = 1.0 / den[:, part * 128 : (part + 1) * 128]
            if t == 1:
                for copy in edge_copies(0, c, ALL):
                    copy.wait_send()

            @pl.loop(0, J // 4)
            def _(b4):
                lane = lane_iota((BM, 128))
                for m0 in range(0, M, BM):
                    rows = pl.ds(m0, BM)
                    found = share[rows, :]
                    for i in range(4):
                        j = 4 * b4 + i
                        probs = [ex[j, part, rows, :] * rden[part, rows, :] for part in range(NP)]
                        folded = probs[0]
                        for prob in probs[1:]:
                            folded = folded + prob
                        found = found + jnp.where(lane == j, jnp.sum(folded, axis=1, keepdims=True), 0.0)
                        if not last:
                            for part, prob in enumerate(probs):
                                lanes = pl.ds(part * 128, 128)
                                st[1 - b, c, j, pl.ds(m0 // TC, BM // TC), :, lanes] = (
                                    (prob * spill_ref[j]).astype(BF16).reshape(BM // TC, TC, 128)
                                )
                    share[rows, :] = found
                if not last:
                    for pair in range(2):
                        for side, first in ((0, 0), (1, TC - 1)):
                            at = pl.ds(first, TR, stride=TC)
                            cols = []
                            for j in (4 * b4 + 2 * pair, 4 * b4 + 2 * pair + 1):
                                for part in range(NP):
                                    cols.append(ex[j, part, at, :] * rden[part, at, :] * spill_ref[j])
                            cs[t + 1, c, side, 2 * b4 + pair] = jnp.concatenate(
                                [jnp.concatenate(cols[:NP], axis=1), jnp.concatenate(cols[NP:], axis=1)], axis=0
                            ).astype(BF16)

            if not last:
                @pl.when(c == 0)
                def _():
                    for copy in edge_copies(t + 1, 0, ALL[:1]):
                        copy.start()

        log_share = jnp.log(jnp.where(real, share[...] * (1.0 / R), 1.0))
        residual = jnp.where(real, zobs[...] - log_share, 0.0)
        if not last:
            send_small(t + 1, residual)
        gap = jnp.max(jnp.max(jnp.abs(residual), axis=0, keepdims=True), axis=1, keepdims=True)

        def meanwhile():
            if not last:
                for copy in edge_copies(t + 1, 0, ALL[1:2]):
                    copy.start()
            if last:
                for row in range(TR):
                    log_out[:, row, :] = exact_dot(
                        eye_wide, log_share[row * TC : (row + 1) * TC], ((1,), (1,))
                    )

        def afterwards():
            if not last:
                for copy in edge_copies(t + 1, 0, ALL[2:]):
                    copy.start()
                for c in range(1, NC):
                    for copy in edge_copies(t + 1, c, ALL):
                        copy.start()

        best = largest(t, jnp.broadcast_to(gap, (1, 128)), meanwhile, afterwards)
        gap_out[t] = jnp.max(best)
        step = step_level / (best + gap_eps)
        mean_now = zmean[...] + step * residual
        if not last:
            zmean[...] = mean_now
            for copy in small_copies(t + 1):
                copy.wait()
            mh_r[...] = mh_r[...] + step * hz_r[t + 1]
            mh_c[...] = mh_c[...] + step * hz_c[t + 1]
        else:
            for row in range(TR):
                mean_out[:, row, :] = exact_dot(
                    eye_wide, mean_now[row * TC : (row + 1) * TC], ((1,), (1,))
                )

    for t in range(ITERS):
        for d in range(1, NX):
            pltpu.make_async_remote_copy(
                src_ref=mxs.at[t, 0], dst_ref=mxg.at[t, gx], send_sem=sg_sem.at[t, d],
                recv_sem=rg_sem.at[t, gx], device_id={"gx": lax.rem(gx + d, NX)}, device_id_type=MESH,
            ).wait_send()
        for d in range(1, NY):
            pltpu.make_async_remote_copy(
                src_ref=mxs.at[t, 1], dst_ref=mxy.at[t, gy], send_sem=sy_sem.at[t, d],
                recv_sem=ry_sem.at[t, gy], device_id={"gy": lax.rem(gy + d, NY)}, device_id_type=MESH,
            ).wait_send()
    for e in range(1, ITERS):
        @pl.loop(0, NC)
        def _(c):
            for copy in edge_copies(e, c, ALL):
                copy.wait_send()


def put_out(mean_ref, log_ref, gap_ref, mean_out, log_out, gap_out):
    mean_out[...] = mean_ref[...]
    log_out[...] = log_ref[...]
    for t in range(ITERS):
        gap_out[t] = gap_ref[t]


def local(*args):
    vmem = pl.BlockSpec(memory_space=pltpu.VMEM)
    smem = pl.BlockSpec(memory_space=pltpu.SMEM)
    anyspace = pl.BlockSpec(memory_space=pl.ANY)
    dma = pltpu.SemaphoreType.DMA
    small = jax.ShapeDtypeStruct((J, TR, TC), F32)
    out_shape = (small, small, jax.ShapeDtypeStruct((ITERS,), F32))
    found = pl.pallas_call(
        kernel,
        out_shape=out_shape,
        in_specs=[anyspace] * 4 + [smem, anyspace, smem, smem, anyspace],
        out_specs=(vmem, vmem, smem),
        scratch_shapes=[
            pltpu.VMEM((2, NC, J, TR, TC, RC), BF16),
            pltpu.VMEM((ITERS, NC, 2, J, TC, RC), BF16),
            pltpu.VMEM((ITERS, NC, 2, J // 2, 2 * TR, RC), BF16),
            pltpu.VMEM((ITERS, NC, 2, J // 2, 2 * TR, RC), BF16),
            pltpu.VMEM((J, NP, M, 128), F32),
            pltpu.VMEM((M, RC), F32),
            pltpu.VMEM((NP, M, 128), F32),
            pltpu.VMEM((2, HM, 256), F32),
            pltpu.VMEM((2, HM, 128), BF16),
            pltpu.VMEM((4, 2, HM, 128), F32),
            pltpu.VMEM((J, 2, HM, 128), BF16),
            pltpu.VMEM((J // 4, M, 128), F32),
            pltpu.VMEM((32, R), BF16),
            pltpu.VMEM((4, M, 128), F32),
            pltpu.VMEM((M, 128), F32),
            pltpu.VMEM((M, 128), F32),
            pltpu.VMEM((M, RC), F32),
            pltpu.VMEM((K, J, TR, TC), F32),
            pltpu.VMEM((J, TR, TC), F32),
            pltpu.VMEM((J, TR, TC), F32),
            pltpu.VMEM((K, R), F32),
            pltpu.VMEM((4, TR, TC), jnp.int32),
            dma((4,)),
            pltpu.VMEM((M, 128), F32),
            pltpu.VMEM((M, 128), F32),
            pltpu.VMEM((ITERS, M, 128), F32),
            pltpu.VMEM((ITERS, 2, TR, 128), F32),
            pltpu.VMEM((ITERS, 2, TC, 128), F32),
            pltpu.VMEM((ITERS, 2, TR, 128), F32),
            pltpu.VMEM((2, TC, 128), F32),
            pltpu.VMEM((2, TR, 128), F32),
            pltpu.VMEM((M, 128), F32),
            pltpu.VMEM((ITERS, 2, 1, 128), F32),
            pltpu.VMEM((ITERS, NX, 1, 128), F32),
            pltpu.VMEM((ITERS, NY, 1, 128), F32),
            dma((NC,)),
            dma,
            dma((ITERS, NC, len(CUTS) - 1, 4)),
            dma((ITERS, NC, len(CUTS) - 1, 4)),
            dma((ITERS, 4)),
            dma((ITERS, 4)),
            dma((ITERS, NX)),
            dma((ITERS, NX)),
            dma((ITERS, NY)),
            dma((ITERS, NY)),
        ],
        compiler_params=pltpu.CompilerParams(
            collective_id=0, has_side_effects=True, vmem_limit_bytes=62 * 1024 * 1024
        ),
    )(*args)
    return pl.pallas_call(
        put_out, out_shape=out_shape, in_specs=[vmem, vmem, smem], out_specs=(vmem, vmem, smem)
    )(*found)


def solution(mesh):
    tile = P(None, "gy", "gx")
    placed = (
        tile, tile, P(None, None, "gy", "gx"), P(), P(), P(None, "gy", "gx", None), P(), P(), tile,
    )
    return jax.shard_map(
        local, mesh=mesh, in_specs=placed, out_specs=(tile, tile, P()), check_vma=False
    )
```
